32 devices in a mesh: groups: 2 (over y), dp: 8 (over z, x), tensor: 2 (over core).
Axes of the slice: x: 2, y: 2, z: 4, core: 2. Of those that a mesh axis runs over, the one named last changes fastest.
Arguments:
- xbc: bfloat16 [2048, 9216], P(('groups', 'dp', 'tensor')), parts along dimension 0, may hold values from -6 to 6
- gate_z: bfloat16 [2048, 8192], P(('groups', 'dp', 'tensor')), parts along dimension 0, may hold values from -6 to 6
- dt_raw: bfloat16 [2048, 128], P(('groups', 'dp', 'tensor')), parts along dimension 0, may hold values from -6 to 6
- conv_weight: float32 [4, 9216], replicated, may hold values from -3 to 3
- conv_bias: float32 [9216], replicated, may hold values from -3 to 3
- dt_bias: float32 [128], P('tensor'), may hold values from -4 to -1
- decay_rate: float32 [128], P('tensor'), may hold values from 0.02 to 2
- d_skip: float32 [128], P('tensor'), may hold values from 0.5 to 2
- norm_gain: float32 [8192], P('tensor'), may hold values from 0.5 to 1.5
- ssm_store: bfloat16 [16, 128, 64, 128], P(('groups', 'dp'), 'tensor'), parts along dimension 0, may hold values from -1.1953125 to 1.1953125
- conv_store: bfloat16 [16, 3, 9216], P(('groups', 'dp'), None, 'tensor'), parts along dimension 0, may hold values from -6 to 6
- source_of: int32 [16], P('groups'), parts along dimension 0, may hold values from 0 to 7, each once
- prefix_len: int32 [16], P(('groups', 'dp')), parts along dimension 0, may hold values from 0 to 8192, as said below
- span_len: int32 [16], P(('groups', 'dp')), parts along dimension 0, may hold values from 32 to 128
Outputs:
- mixed: bfloat16 [2048, 8192], P(('groups', 'dp'), 'tensor'), parts along dimension 0
The draws below stay inside these ranges and needn't reach their ends.
There are 2 independent parts, one for each index of `groups`. The reference program is written for one: setup_inputs(seed, part) draws one part's arguments, and reference() takes and returns one part's arrays. A program takes and returns all parts, laid end to end along the dimension named above; an argument that names none is the same for every part. Nothing has to cross between parts.
Inputs may be any that keep to these rules, and one draw needn't show every extreme that they name: `source_of`: each of 0 to 7 appears once. `prefix_len`: 0 marks a request without kept states.
All inputs are finite; a program needn't handle non-finite values.
Results may differ from the reference program's by a relative error of at most 0.0045.
Values may be sent and summed in bfloat16 or wider, within the bound.
No kernel may reach another device: no remote copies, remote signals or barrier semaphores. Data moves between devices by JAX's collectives and lax.ppermute only.
A program may use at most 64 MiB of HBM per device.

```python
import math
import jax
import jax.numpy as jnp
from jax import lax

HEADS = 128
HEAD_DIM = 64
STATE = 128
GROUPS = 4
NORM_WIDTH = 2048
KCONV = 4
PREFIX_MAX = 8192
TOK_DEV = 128
REQS = 8
TOKENS = 1024
INNER = 8192
CONV_CH = 9216
CONV_HALF = 4608


def draw_prefix_len(key, part):
    key_len, key_fresh = jax.random.split(jax.random.fold_in(key, 11))
    lengths = jax.random.randint(key_len, (REQS,), 1, PREFIX_MAX + 1)
    fresh = jax.random.randint(key_fresh, (REQS,), 0, 4) == 0
    lengths = jnp.where(fresh, 0, lengths)
    index = jnp.arange(REQS)
    lengths = jnp.where(index == 0, PREFIX_MAX, lengths)
    lengths = jnp.where(index == 1, 0, lengths)
    return lengths.astype(jnp.int32)


def draw_span_len(key, part):
    lengths = jax.random.randint(jax.random.fold_in(key, 23), (REQS,), TOK_DEV // 4, TOK_DEV + 1)
    index = jnp.arange(REQS)
    lengths = jnp.where(index == 0, TOK_DEV, lengths)
    return lengths.astype(jnp.int32)


def block_levels(stream_key, dims, cuts, low, top_value):
    def one(position, shards_of):
        heights = jax.random.uniform(jax.random.fold_in(jax.random.fold_in(stream_key, 6), position), (shards_of,), jnp.float32, low / len(cuts), top_value / len(cuts))
        return jnp.repeat(jnp.exp(heights), dims[position] // shards_of).reshape((-1,) + (1,) * (len(dims) - position - 1))

    factor_of = one(*cuts[0])
    for cut in cuts[1:]:
        factor_of = factor_of * one(*cut)
    return factor_of


def scatter_about(own_key, dims, deviation, limit, shards=(), kind=jnp.bfloat16):
    values = jax.random.normal(own_key, dims, jnp.float32) * deviation
    if len(shards) > 0:
        values = block_levels(own_key, dims, shards, -0.22, 0.18) * values
    return jnp.clip(values, min=-limit, max=limit).astype(kind)


def setup_inputs(seed: int = 0, part: int = 0) -> dict:
    seeds = jax.random.split(jax.random.key(seed), 15)
    part_splits = jax.random.split(jax.random.fold_in(seeds[14], part), 15)
    return {
        "xbc": scatter_about(part_splits[0], (TOKENS, CONV_CH), 1.0, 6.0, ((0, 16),)),
        "gate_z": scatter_about(part_splits[1], (TOKENS, INNER), 1.0, 6.0, ((0, 16),)),
        "dt_raw": scatter_about(part_splits[2], (TOKENS, HEADS), 1.0, 6.0, ((0, 16),)),
        "conv_weight": scatter_about(seeds[3], (KCONV, CONV_CH), KCONV ** -0.5, 3.0, (), jnp.float32),
        "conv_bias": scatter_about(seeds[4], (CONV_CH,), 0.5, 3.0, (), jnp.float32),
        "dt_bias": jnp.clip(-4.0 + 3.0 * jax.random.uniform(seeds[5], (HEADS,), jnp.float32) ** block_levels(seeds[5], (HEADS,), ((0, 2),), -0.2, 0.2), -4.0, -1.0),
        "decay_rate": jnp.clip(jnp.exp(math.log(2.0) - 4.6051702 * jax.random.uniform(seeds[6], (HEADS,), jnp.float32) ** block_levels(seeds[6], (HEADS,), ((0, 2),), -0.2, 0.2)), 0.02, 2.0),
        "d_skip": jnp.clip(0.5 + 1.5 * jax.random.uniform(seeds[7], (HEADS,), jnp.float32) ** block_levels(seeds[7], (HEADS,), ((0, 2),), -0.2, 0.2), 0.5, 2.0),
        "norm_gain": jnp.clip(1.0 + 0.1 * jax.random.normal(seeds[8], (INNER,), jnp.float32), 0.5, 1.5),
        "ssm_store": scatter_about(part_splits[9], (REQS, HEADS, HEAD_DIM, STATE), 0.2, 1.1953125, ((0, 8), (1, 2))),
        "conv_store": scatter_about(part_splits[10], (REQS, KCONV - 1, CONV_CH), 1.0, 6.0, ((0, 8), (2, 2))),
        "source_of": jax.random.permutation(part_splits[11], REQS).astype(jnp.int32),
        "prefix_len": draw_prefix_len(jax.random.fold_in(jax.random.fold_in(seeds[14], part), 71), part),
        "span_len": draw_span_len(jax.random.fold_in(jax.random.fold_in(seeds[14], part), 71), part),
    }


EPSILON = 1e-05

def convolve(rims, rows, weight, bias):
    extended = jnp.concatenate([rims, rows], axis=0).astype(jnp.float32)
    count = rows.shape[0]
    total = bias[None, :]
    for offset in range(weight.shape[0]):
        total = total + weight[offset][None, :] * extended[offset:offset + count]
    return jax.nn.silu(total).astype(jnp.bfloat16)

def state_space(activated, gate_rows, dt_rows, dt_bias, decay_rate, d_skip, norm_gain, kept_state, live_rows):
    count = activated.shape[0]
    heads = dt_bias.shape[0]
    inner = heads * HEAD_DIM
    groups = (activated.shape[1] - inner) // (2 * STATE)
    per_group = heads // groups
    x_heads = activated[:, :inner].reshape(count, heads, HEAD_DIM).astype(jnp.float32)
    b_proj = activated[:, inner:inner + groups * STATE].reshape(count, groups, STATE).astype(jnp.float32)
    c_proj = activated[:, inner + groups * STATE:].reshape(count, groups, STATE).astype(jnp.float32)
    step_size = jax.nn.softplus(dt_rows.astype(jnp.float32) + dt_bias[None, :])
    cumulative = jnp.cumsum(-decay_rate[None, :] * step_size, axis=0)
    scores = jnp.einsum('tgn,ugn->gtu', c_proj, b_proj)
    spread = cumulative.T[:, :, None] - cumulative.T[:, None, :]
    causal = jnp.arange(count, dtype=jnp.int32)[:, None] >= jnp.arange(count, dtype=jnp.int32)[None, :]
    decay = jnp.where(causal, jnp.exp(jnp.where(causal, spread, 0.0)), 0.0)
    weights = decay.reshape(groups, per_group, count, count) * scores[:, None] * step_size.T.reshape(groups, per_group, 1, count)
    weights = weights.reshape(heads, count, count).astype(jnp.bfloat16)
    intra = jnp.einsum('htu,uhp->thp', weights.astype(jnp.float32), x_heads)
    state_full = kept_state.astype(jnp.float32).reshape(groups, per_group, HEAD_DIM, STATE)
    carried = jnp.einsum('tgn,gkpn->tgkp', c_proj, state_full)
    carried = carried.reshape(count, heads, HEAD_DIM) * jnp.exp(cumulative)[:, :, None]
    mixed = intra + carried + d_skip[None, :, None] * x_heads
    gated = mixed.reshape(count, inner) * jax.nn.silu(gate_rows.astype(jnp.float32))
    grouped = gated.reshape(count, inner // NORM_WIDTH, NORM_WIDTH)
    scale = lax.rsqrt(lax.optimization_barrier(jnp.mean(grouped * grouped, axis=-1, keepdims=True)) + EPSILON)
    normed = (grouped * scale).reshape(count, inner) * norm_gain[None, :]
    return jnp.where(live_rows[:, None], normed, 0.0).astype(jnp.bfloat16)

def reference(xbc, gate_z, dt_raw, conv_weight, conv_bias, dt_bias, decay_rate, d_skip, norm_gain, ssm_store, conv_store, source_of, prefix_len, span_len):
    x_width = HEADS // 2 * HEAD_DIM
    b_width = GROUPS // 2 * STATE
    xbc_req = xbc.reshape(REQS, TOK_DEV, CONV_CH)
    gate_req = gate_z.reshape(REQS, TOK_DEV, INNER)
    dt_req = dt_raw.reshape(REQS, TOK_DEV, HEADS)

    def reorder(rows):
        halves = rows.reshape(rows.shape[0], 2, CONV_HALF)
        x_part = halves[:, :, :x_width].reshape(rows.shape[0], INNER)
        b_part = halves[:, :, x_width:x_width + b_width].reshape(rows.shape[0], GROUPS * STATE)
        c_part = halves[:, :, x_width + b_width:].reshape(rows.shape[0], GROUPS * STATE)
        return jnp.concatenate([x_part, b_part, c_part], axis=1)

    def serve(index):
        source = source_of[index]
        live = prefix_len[index] > 0
        state = jnp.where(live, ssm_store[source], jnp.zeros_like(ssm_store[source]))
        rims = jnp.where(live, conv_store[source], jnp.zeros_like(conv_store[source]))
        activated = convolve(rims, xbc_req[index], conv_weight, conv_bias)
        live_rows = jnp.arange(TOK_DEV, dtype=jnp.int32) < span_len[index]
        return state_space(reorder(activated), gate_req[index], dt_req[index], dt_bias, decay_rate, d_skip, norm_gain, state, live_rows)
    outputs = lax.map(serve, jnp.arange(REQS, dtype=jnp.int32))
    return outputs.reshape(TOKENS, INNER)
```

```python
import functools

import jax
import jax.numpy as jnp
from jax import lax
from jax.experimental import pallas as pl
from jax.experimental.pallas import tpu as pltpu
from jax.sharding import PartitionSpec as P

HEAD_DIM = 64
STATE = 128
NORM_WIDTH = 2048
EPSILON = 1e-05
LANES = 128
DIRECT_MAX = 8


def swap(value, axis, offset):
    count = lax.axis_size(axis)
    return lax.ppermute(value, axis, [(i, i ^ offset) for i in range(count)])


def offsets(count):
    return sorted(range(1, count), key=lambda k: (-(k.bit_length()), k))


def main_kernel(
    core_ref,
    live_ref,
    skip_ref,
    own_x,
    peer_x,
    own_bc,
    peer_bc,
    weight_x,
    weight_bc,
    bias_x,
    bias_bc,
    rims_x,
    rims_bc,
    own_gate,
    peer_gate,
    own_dt,
    peer_dt,
    head_rows,
    intra_out,
    carry_out,
    c_out,
    extended,
    scores,
    columns,
    cum_rows,
    step_rows,
):
    block = pl.program_id(0)
    count = 2 * own_x.shape[0]
    half = own_x.shape[0]
    width = own_x.shape[1]
    per_block = width // HEAD_DIM
    groups = c_out.shape[1] // STATE
    blocks = pl.num_programs(0)
    first = core_ref[0] == 0
    live = live_ref[0] > 0
    taps = weight_x.shape[0]
    pad = 8 - (taps - 1)

    def whole(own, peer):
        mine = own[...].astype(jnp.float32)
        other = peer[...].astype(jnp.float32)
        return jnp.where(first, mine, other), jnp.where(first, other, mine)

    def convolve(own, peer, rims, weight, bias):
        low, high = whole(own, peer)
        edge = rims[...].astype(jnp.float32)
        extended[pad:8, :] = jnp.where(live, edge, jnp.zeros_like(edge))
        extended[8 : 8 + half, :] = low
        extended[8 + half : 8 + count, :] = high
        total = jnp.broadcast_to(bias[...], (count, width))
        for k in range(taps):
            total = total + weight[k : k + 1, :] * extended[pad + k : pad + k + count, :]
        return jax.nn.silu(total).astype(jnp.bfloat16)

    row = lax.broadcasted_iota(jnp.int32, (count, LANES), 0)
    lane = lax.broadcasted_iota(jnp.int32, (count, LANES), 1)

    @pl.when(block == 0)
    def _():
        active = convolve(own_bc, peer_bc, rims_bc, weight_bc, bias_bc)
        c_out[...] = active[:, groups * STATE :]
        for g in range(groups):
            b = active[:, g * STATE : (g + 1) * STATE]
            c = active[:, (groups + g) * STATE : (groups + g + 1) * STATE]
            product = lax.dot_general(
                c, b, (((1,), (1,)), ((), ())), preferred_element_type=jnp.float32
            )
            scores[g] = jnp.where(row >= lane, product, 0.0)
        low, high = whole(own_dt, peer_dt)
        raw = jnp.concatenate([low, high], axis=0)
        raw = jnp.where(first, raw, pltpu.roll(raw, LANES // 2, 1))
        step = jax.nn.softplus(raw + head_rows[0:1, :])
        total = -head_rows[1:2, :] * step
        shift = 1
        while shift < count:
            total = total + jnp.where(row >= shift, pltpu.roll(total, shift, 0), 0.0)
            shift *= 2
        cum_rows[...] = total.T
        step_rows[...] = step.T
        for i in range(columns.shape[0]):
            columns[i] = total[:, i * per_block : (i + 1) * per_block]

    active = convolve(own_x, peer_x, rims_x, weight_x, bias_x)
    low, high = whole(own_gate, peer_gate)
    gate = jax.nn.silu(jnp.concatenate([low, high], axis=0))
    score = scores[block // (blocks // groups)]
    column = columns[block]
    at = pl.multiple_of(block * per_block, per_block)
    cum_row = cum_rows[pl.ds(at, per_block), :]
    step_row = step_rows[pl.ds(at, per_block), :]
    left = lane < HEAD_DIM
    scale = jnp.where(live, 1.0, 0.0)
    for pair in range(per_block // 2):
        spread, weights = [], []
        for j in (2 * pair, 2 * pair + 1):
            cum = jnp.broadcast_to(column[:, j : j + 1], (count, LANES))
            decay = jnp.exp(jnp.minimum(cum - cum_row[j : j + 1, :], 0.0))
            weights.append((decay * score * step_row[j : j + 1, :]).astype(jnp.bfloat16))
            spread.append(cum)
        lanes = slice(pair * LANES, (pair + 1) * LANES)
        x = active[:, lanes]
        zero = jnp.zeros_like(x)
        stacked = jnp.concatenate([jnp.where(left, x, zero), jnp.where(left, zero, x)], axis=0)
        intra = lax.dot_general(
            jnp.concatenate(weights, axis=1),
            stacked,
            (((1,), (0,)), ((), ())),
            preferred_element_type=jnp.float32,
        )
        skip = jnp.where(left, skip_ref[at + 2 * pair], skip_ref[at + 2 * pair + 1])
        gates = gate[:, lanes]
        intra_out[:, lanes] = (intra + skip * x.astype(jnp.float32)) * gates
        decayed = jnp.exp(jnp.where(left, spread[0], spread[1]))
        carry_out[:, lanes] = gates * decayed * scale


def main_stage(core, live, d_skip, xbc, peer_xbc, weight, bias, rims, gate, peer_gate, dt, peer_dt, heads):
    rows, channels = xbc.shape
    half = channels // 2
    count = 2 * rows
    inner = gate.shape[1] // 2
    width = half - inner
    groups = width // (2 * STATE)
    blocks = inner // width
    per_half = half // width
    per_inner = inner // width
    at_x = lambda i, core, *_: (0, core[0] * per_half + i)
    at_bc = lambda i, core, *_: (0, core[0] * per_half + blocks)
    at_gate = lambda i, core, *_: (0, core[0] * per_inner + i)
    fixed = lambda i, *_: (0, 0)
    step = lambda i, *_: (0, i)
    last = lambda i, *_: (0, blocks)
    taps = weight.shape[0]
    token = lambda index: pl.BlockSpec((rows, width), index)
    grid_spec = pltpu.PrefetchScalarGridSpec(
        num_scalar_prefetch=3,
        grid=(blocks,),
        in_specs=[
            token(at_x),
            token(at_x),
            token(at_bc),
            token(at_bc),
            pl.BlockSpec((taps, width), at_x),
            pl.BlockSpec((taps, width), at_bc),
            pl.BlockSpec((1, width), at_x),
            pl.BlockSpec((1, width), at_bc),
            pl.BlockSpec((taps - 1, width), step),
            pl.BlockSpec((taps - 1, width), last),
            token(at_gate),
            token(at_gate),
            pl.BlockSpec((rows, LANES), fixed),
            pl.BlockSpec((rows, LANES), fixed),
            pl.BlockSpec((8, LANES), fixed),
        ],
        out_specs=[
            pl.BlockSpec((count, width), step),
            pl.BlockSpec((count, width), step),
            pl.BlockSpec((count, groups * STATE), fixed),
        ],
        scratch_shapes=[
            pltpu.VMEM((count + 8, width), jnp.float32),
            pltpu.VMEM((groups, count, LANES), jnp.float32),
            pltpu.VMEM((blocks, count, width // HEAD_DIM), jnp.float32),
            pltpu.VMEM((LANES, count), jnp.float32),
            pltpu.VMEM((LANES, count), jnp.float32),
        ],
    )
    return pl.pallas_call(
        main_kernel,
        grid_spec=grid_spec,
        out_shape=[
            jax.ShapeDtypeStruct((count, inner), jnp.float32),
            jax.ShapeDtypeStruct((count, inner), jnp.float32),
            jax.ShapeDtypeStruct((count, groups * STATE), jnp.bfloat16),
        ],
        compiler_params=pltpu.CompilerParams(vmem_limit_bytes=16 << 20),
        cost_estimate=pl.CostEstimate(flops=400_000_000, bytes_accessed=8_000_000, transcendentals=2_000_000),
        name="main_stage",
    )(core, live, d_skip, xbc, peer_xbc, xbc, peer_xbc, weight, weight, bias, bias, rims, rims, gate, peer_gate, dt, peer_dt, heads)


def tail_kernel(count_pieces, turn_ref, span_ref, *refs):
    pieces = refs[:count_pieces]
    intra, carry, c_proj, gain, out, state, sems = refs[count_pieces:]
    copies = []
    for k, piece in enumerate(pieces):
        slot = turn_ref[0] ^ k
        copy = pltpu.make_async_copy(piece, state.at[slot], sems.at[k])
        copy.start()
        copies.append(copy)
    for copy in copies:
        copy.wait()
    tokens, inner = intra.shape
    groups = c_proj.shape[1] // STATE
    rows = state.shape[1]
    width = inner // groups
    norms = width // NORM_WIDTH
    per_group = width // rows if rows <= width else 1
    keep = lax.broadcasted_iota(jnp.int32, (tokens, 1), 0) < span_ref[0]
    chunk = min(rows, 512)
    for n in range(inner // NORM_WIDTH):
        g = n // norms
        c = c_proj[:, g * STATE : (g + 1) * STATE]
        gated = []
        total = jnp.zeros((tokens, 1), jnp.float32)
        for at in range(n * NORM_WIDTH, (n + 1) * NORM_WIDTH, chunk):
            part = state[at // rows, at % rows : at % rows + chunk, :]
            carried = lax.dot_general(
                c, part, (((1,), (1,)), ((), ())), preferred_element_type=jnp.float32
            )
            lanes = slice(at, at + chunk)
            value = intra[:, lanes] + carry[:, lanes] * carried
            total = total + jnp.sum(value * value, axis=1, keepdims=True)
            gated.append((lanes, value))
        scale = lax.rsqrt(total * (1.0 / NORM_WIDTH) + EPSILON)
        for lanes, value in gated:
            normed = value * scale * gain[:, lanes]
            out[:, lanes] = jnp.where(keep, normed, 0.0).astype(jnp.bfloat16)


def tail_stage(turn, span_len, pieces, intra, carry, c_proj, gain):
    rows = pieces[0].shape[0]
    vmem = pl.BlockSpec(memory_space=pltpu.VMEM)
    grid_spec = pltpu.PrefetchScalarGridSpec(
        num_scalar_prefetch=2,
        grid=(),
        in_specs=[pl.BlockSpec(memory_space=pl.ANY)] * len(pieces) + [vmem] * 4,
        out_specs=vmem,
        scratch_shapes=[
            pltpu.VMEM((len(pieces), rows, STATE), jnp.bfloat16),
            pltpu.SemaphoreType.DMA((len(pieces),)),
        ],
    )
    return pl.pallas_call(
        functools.partial(tail_kernel, len(pieces)),
        grid_spec=grid_spec,
        out_shape=jax.ShapeDtypeStruct(intra.shape, jnp.bfloat16),
        compiler_params=pltpu.CompilerParams(vmem_limit_bytes=24 << 20),
        cost_estimate=pl.CostEstimate(flops=140_000_000, bytes_accessed=6_000_000, transcendentals=0),
        name="tail_stage",
    )(turn, span_len, *pieces, intra, carry, c_proj, gain)


def gather_rims(conv_store, source_of, me):
    count = lax.axis_size("dp")
    held = conv_store
    index = jnp.zeros((), jnp.int32)
    away = source_of[me] ^ me
    bit = count // 2
    place = 1
    while bit > 0:
        held = jnp.concatenate([held, swap(held, "dp", bit)], axis=0)
        index = index + place * ((away // bit) & 1)
        bit //= 2
        place *= 2
    return lax.dynamic_index_in_dim(held, index, 0, keepdims=False)


def local(
    xbc,
    gate_z,
    dt_raw,
    conv_weight,
    conv_bias,
    dt_bias,
    decay_rate,
    d_skip,
    norm_gain,
    ssm_store,
    conv_store,
    source_of,
    prefix_len,
    span_len,
):
    me = lax.axis_index("dp")
    owners = lax.axis_size("dp")
    core = lax.axis_index("tensor").astype(jnp.int32).reshape(1)
    direct = owners <= DIRECT_MAX
    order = offsets(owners)
    state = ssm_store.reshape(owners, -1, STATE)
    if direct:
        held = [None] * owners
        for k in order:
            held[k] = swap(state[k], "dp", k)
        held[0] = state[0]
    else:
        held = lax.all_to_all(state, "dp", split_axis=0, concat_axis=0, tiled=True)

    peer_xbc = swap(xbc, "tensor", 1)
    peer_gate = swap(gate_z, "tensor", 1)
    peer_dt = swap(dt_raw, "tensor", 1)
    rims = gather_rims(conv_store, source_of, me)
    heads = jnp.pad(jnp.stack([dt_bias, decay_rate]), ((0, 6), (0, LANES - dt_bias.shape[0])))
    intra, carry, c_proj = main_stage(
        core,
        prefix_len,
        d_skip,
        xbc,
        peer_xbc,
        conv_weight,
        conv_bias.reshape(1, -1),
        rims,
        gate_z,
        peer_gate,
        dt_raw,
        peer_dt,
        heads,
    )

    if direct:
        stacked = jnp.stack(held)
        got = [None] * owners
        for k in order + [0]:
            pick = lax.dynamic_index_in_dim(stacked, me ^ source_of[me ^ k], 0, keepdims=False)
            got[k] = swap(pick, "dp", k) if k else pick
        turn = source_of[me] ^ me
    else:
        picked = jnp.take(held, source_of, axis=0)
        arrived = lax.all_to_all(picked, "dp", split_axis=0, concat_axis=0, tiled=True)
        got = [arrived.reshape(-1, STATE)]
        turn = jnp.zeros((), jnp.int32)
    return tail_stage(
        turn.astype(jnp.int32).reshape(1),
        span_len,
        got,
        intra,
        carry,
        c_proj,
        norm_gain.reshape(1, -1),
    )


def solution(mesh):
    in_specs = (
        P(("groups", "dp", "tensor"), None),
        P(("groups", "dp", "tensor"), None),
        P(("groups", "dp", "tensor"), None),
        P(),
        P(),
        P("tensor"),
        P("tensor"),
        P("tensor"),
        P("tensor"),
        P(("groups", "dp"), "tensor", None, None),
        P(("groups", "dp"), None, "tensor"),
        P("groups"),
        P(("groups", "dp")),
        P(("groups", "dp")),
    )
    out_specs = P(("groups", "dp"), "tensor")
    return jax.shard_map(local, mesh=mesh, in_specs=in_specs, out_specs=out_specs, check_vma=False)
```

```python
import functools

import jax
import jax.numpy as jnp
from jax import lax
from jax.experimental import pallas as pl
from jax.experimental.pallas import tpu as pltpu
from jax.sharding import PartitionSpec as P


HEAD_DIM = 64
STATE = 128
NORM_WIDTH = 2048
EPSILON = 1e-05
LANES = 128
DIRECT_MAX = 8


def swap(value, axis, offset):
    count = lax.axis_size(axis)
    return lax.ppermute(value, axis, [(i, i ^ offset) for i in range(count)])


def offsets(count):
    return sorted(range(1, count), key=lambda k: (-(k.bit_length()), k))


def main_kernel(
    core_ref,
    live_ref,
    skip_ref,
    own_x,
    peer_x,
    own_bc,
    peer_bc,
    weight_x,
    weight_bc,
    bias_x,
    bias_bc,
    rims_x,
    rims_bc,
    own_gate,
    peer_gate,
    own_dt,
    peer_dt,
    head_rows,
    intra_out,
    carry_out,
    c_out,
    extended,
    scores,
    columns,
    cum_rows,
    step_rows,
):
    block = pl.program_id(0)
    count = 2 * own_x.shape[0]
    half = own_x.shape[0]
    width = own_x.shape[1]
    per_block = width // HEAD_DIM
    groups = c_out.shape[1] // STATE
    blocks = pl.num_programs(0)
    first = core_ref[0] == 0
    live = live_ref[0] > 0
    taps = weight_x.shape[0]
    pad = 8 - (taps - 1)

    def whole(own, peer):
        mine = own[...].astype(jnp.float32)
        other = peer[...].astype(jnp.float32)
        return jnp.where(first, mine, other), jnp.where(first, other, mine)

    def convolve(own, peer, rims, weight, bias):
        low, high = whole(own, peer)
        edge = rims[...].astype(jnp.float32)
        extended[pad:8, :] = jnp.where(live, edge, jnp.zeros_like(edge))
        extended[8 : 8 + half, :] = low
        extended[8 + half : 8 + count, :] = high
        total = jnp.broadcast_to(bias[...], (count, width))
        for k in range(taps):
            total = total + weight[k : k + 1, :] * extended[pad + k : pad + k + count, :]
        return jax.nn.silu(total).astype(jnp.bfloat16)

    row = lax.broadcasted_iota(jnp.int32, (count, LANES), 0)
    lane = lax.broadcasted_iota(jnp.int32, (count, LANES), 1)

    @pl.when(block == 0)
    def _():
        active = convolve(own_bc, peer_bc, rims_bc, weight_bc, bias_bc)
        c_out[...] = active[:, groups * STATE :]
        for g in range(groups):
            b = active[:, g * STATE : (g + 1) * STATE]
            c = active[:, (groups + g) * STATE : (groups + g + 1) * STATE]
            product = lax.dot_general(
                c, b, (((1,), (1,)), ((), ())), preferred_element_type=jnp.float32
            )
            scores[g] = jnp.where(row >= lane, product, 0.0)
        low, high = whole(own_dt, peer_dt)
        raw = jnp.concatenate([low, high], axis=0)
        raw = jnp.where(first, raw, pltpu.roll(raw, LANES // 2, 1))
        step = jax.nn.softplus(raw + head_rows[0:1, :])
        total = -head_rows[1:2, :] * step
        shift = 1
        while shift < count:
            total = total + jnp.where(row >= shift, pltpu.roll(total, shift, 0), 0.0)
            shift *= 2
        cum_rows[...] = total.T
        step_rows[...] = step.T
        for i in range(columns.shape[0]):
            columns[i] = total[:, i * per_block : (i + 1) * per_block]

    active = convolve(own_x, peer_x, rims_x, weight_x, bias_x)
    low, high = whole(own_gate, peer_gate)
    gate = jax.nn.silu(jnp.concatenate([low, high], axis=0))
    score = scores[block // (blocks // groups)]
    column = columns[block]
    at = pl.multiple_of(block * per_block, per_block)
    cum_row = cum_rows[pl.ds(at, per_block), :]
    step_row = step_rows[pl.ds(at, per_block), :]
    left = lane < HEAD_DIM
    scale = jnp.where(live, 1.0, 0.0)
    for pair in range(per_block // 2):
        spread, weights = [], []
        for j in (2 * pair, 2 * pair + 1):
            cum = jnp.broadcast_to(column[:, j : j + 1], (count, LANES))
            decay = jnp.exp(jnp.minimum(cum - cum_row[j : j + 1, :], 0.0))
            weights.append((decay * score * step_row[j : j + 1, :]).astype(jnp.bfloat16))
            spread.append(cum)
        lanes = slice(pair * LANES, (pair + 1) * LANES)
        x = active[:, lanes]
        zero = jnp.zeros_like(x)
        stacked = jnp.concatenate([jnp.where(left, x, zero), jnp.where(left, zero, x)], axis=0)
        intra = lax.dot_general(
            jnp.concatenate(weights, axis=1),
            stacked,
            (((1,), (0,)), ((), ())),
            preferred_element_type=jnp.float32,
        )
        skip = jnp.where(left, skip_ref[at + 2 * pair], skip_ref[at + 2 * pair + 1])
        gates = gate[:, lanes]
        intra_out[:, lanes] = (intra + skip * x.astype(jnp.float32)) * gates
        decayed = jnp.exp(jnp.where(left, spread[0], spread[1]))
        carry_out[:, lanes] = gates * decayed * scale


def main_stage(core, live, d_skip, xbc, peer_xbc, weight, bias, rims, gate, peer_gate, dt, peer_dt, heads):
    rows, channels = xbc.shape
    half = channels // 2
    count = 2 * rows
    inner = gate.shape[1] // 2
    width = half - inner
    groups = width // (2 * STATE)
    blocks = inner // width
    per_half = half // width
    per_inner = inner // width
    at_x = lambda i, core, *_: (0, core[0] * per_half + i)
    at_bc = lambda i, core, *_: (0, core[0] * per_half + blocks)
    at_gate = lambda i, core, *_: (0, core[0] * per_inner + i)
    fixed = lambda i, *_: (0, 0)
    step = lambda i, *_: (0, i)
    last = lambda i, *_: (0, blocks)
    taps = weight.shape[0]
    token = lambda index: pl.BlockSpec((rows, width), index)
    grid_spec = pltpu.PrefetchScalarGridSpec(
        num_scalar_prefetch=3,
        grid=(blocks,),
        in_specs=[
            token(at_x),
            token(at_x),
            token(at_bc),
            token(at_bc),
            pl.BlockSpec((taps, width), at_x),
            pl.BlockSpec((taps, width), at_bc),
            pl.BlockSpec((1, width), at_x),
            pl.BlockSpec((1, width), at_bc),
            pl.BlockSpec((taps - 1, width), step),
            pl.BlockSpec((taps - 1, width), last),
            token(at_gate),
            token(at_gate),
            pl.BlockSpec((rows, LANES), fixed),
            pl.BlockSpec((rows, LANES), fixed),
            pl.BlockSpec((8, LANES), fixed),
        ],
        out_specs=[
            pl.BlockSpec((count, width), step),
            pl.BlockSpec((count, width), step),
            pl.BlockSpec((count, groups * STATE), fixed),
        ],
        scratch_shapes=[
            pltpu.VMEM((count + 8, width), jnp.float32),
            pltpu.VMEM((groups, count, LANES), jnp.float32),
            pltpu.VMEM((blocks, count, width // HEAD_DIM), jnp.float32),
            pltpu.VMEM((LANES, count), jnp.float32),
            pltpu.VMEM((LANES, count), jnp.float32),
        ],
    )
    return pl.pallas_call(
        main_kernel,
        grid_spec=grid_spec,
        out_shape=[
            jax.ShapeDtypeStruct((count, inner), jnp.float32),
            jax.ShapeDtypeStruct((count, inner), jnp.float32),
            jax.ShapeDtypeStruct((count, groups * STATE), jnp.bfloat16),
        ],
        compiler_params=pltpu.CompilerParams(vmem_limit_bytes=16 << 20),
        cost_estimate=pl.CostEstimate(flops=400_000_000, bytes_accessed=8_000_000, transcendentals=2_000_000),
        name="main_stage",
    )(core, live, d_skip, xbc, peer_xbc, xbc, peer_xbc, weight, weight, bias, bias, rims, rims, gate, peer_gate, dt, peer_dt, heads)


def tail_kernel(count_pieces, turn_ref, span_ref, *refs):
    pieces = refs[:count_pieces]
    intra, carry, c_proj, gain, out, state, sems = refs[count_pieces:]
    copies = []
    for k, piece in enumerate(pieces):
        slot = turn_ref[0] ^ k
        copy = pltpu.make_async_copy(piece, state.at[slot], sems.at[k])
        copy.start()
        copies.append(copy)
    for copy in copies:
        copy.wait()
    tokens, inner = intra.shape
    groups = c_proj.shape[1] // STATE
    rows = state.shape[1]
    width = inner // groups
    norms = width // NORM_WIDTH
    keep = lax.broadcasted_iota(jnp.int32, (tokens, 1), 0) < span_ref[0]
    chunk = min(rows, 512)
    for n in range(inner // NORM_WIDTH):
        g = n // norms
        c = c_proj[:, g * STATE : (g + 1) * STATE]
        gated = []
        total = jnp.zeros((tokens, 1), jnp.float32)
        for at in range(n * NORM_WIDTH, (n + 1) * NORM_WIDTH, chunk):
            part = state[at // rows, at % rows : at % rows + chunk, :]
            carried = lax.dot_general(
                c, part, (((1,), (1,)), ((), ())), preferred_element_type=jnp.float32
            )
            lanes = slice(at, at + chunk)
            value = intra[:, lanes] + carry[:, lanes] * carried
            total = total + jnp.sum(value * value, axis=1, keepdims=True)
            gated.append((lanes, value))
        scale = lax.rsqrt(total * (1.0 / NORM_WIDTH) + EPSILON)
        for lanes, value in gated:
            normed = value * scale * gain[:, lanes]
            out[:, lanes] = jnp.where(keep, normed, 0.0).astype(jnp.bfloat16)


def tail_stage(turn, span_len, pieces, intra, carry, c_proj, gain):
    rows = pieces[0].shape[0]
    vmem = pl.BlockSpec(memory_space=pltpu.VMEM)
    grid_spec = pltpu.PrefetchScalarGridSpec(
        num_scalar_prefetch=2,
        grid=(),
        in_specs=[pl.BlockSpec(memory_space=pl.ANY)] * len(pieces) + [vmem] * 4,
        out_specs=vmem,
        scratch_shapes=[
            pltpu.VMEM((len(pieces), rows, STATE), jnp.bfloat16),
            pltpu.SemaphoreType.DMA((len(pieces),)),
        ],
    )
    return pl.pallas_call(
        functools.partial(tail_kernel, len(pieces)),
        grid_spec=grid_spec,
        out_shape=jax.ShapeDtypeStruct(intra.shape, jnp.bfloat16),
        compiler_params=pltpu.CompilerParams(vmem_limit_bytes=24 << 20),
        cost_estimate=pl.CostEstimate(flops=140_000_000, bytes_accessed=6_000_000, transcendentals=0),
        name="tail_stage",
    )(turn, span_len, *pieces, intra, carry, c_proj, gain)


def cut_kernel(chosen, state, *refs):
    pieces, sems = refs[: len(chosen)], refs[-1]
    copies = []
    for i, (k, piece) in enumerate(zip(chosen, pieces)):
        copy = pltpu.make_async_copy(state.at[k], piece, sems.at[i])
        copy.start()
        copies.append(copy)
    for copy in copies:
        copy.wait()


def cut_stage(state, chosen):
    return pl.pallas_call(
        functools.partial(cut_kernel, chosen),
        in_specs=[pl.BlockSpec(memory_space=pl.ANY)],
        out_specs=[pl.BlockSpec(memory_space=pltpu.VMEM)] * len(chosen),
        out_shape=[jax.ShapeDtypeStruct(state.shape[1:], state.dtype)] * len(chosen),
        scratch_shapes=[pltpu.SemaphoreType.DMA((len(chosen),))],
        compiler_params=pltpu.CompilerParams(vmem_limit_bytes=8 << 20),
        name="cut_stage",
    )(state)


def pick_kernel(order, me_ref, source_ref, *refs):
    count = len(order)
    held, slots = refs[:count], refs[count:]
    for slot, k in zip(slots, order):
        wanted = me_ref[0] ^ source_ref[me_ref[0] ^ k]
        for r in range(count):

            @pl.when(wanted == r)
            def _(slot=slot, r=r):
                slot[...] = held[r][...]


def pick_stage(me, source_of, held, order):
    vmem = pl.BlockSpec(memory_space=pltpu.VMEM)
    grid_spec = pltpu.PrefetchScalarGridSpec(
        num_scalar_prefetch=2,
        grid=(),
        in_specs=[vmem] * len(held),
        out_specs=[vmem] * len(order),
    )
    shape = jax.ShapeDtypeStruct(held[0].shape, held[0].dtype)
    return pl.pallas_call(
        functools.partial(pick_kernel, tuple(order)),
        grid_spec=grid_spec,
        out_shape=[shape] * len(order),
        compiler_params=pltpu.CompilerParams(vmem_limit_bytes=8 << 20),
        name="pick_stage",
    )(me, source_of, *held)


def gather_rims(conv_store, source_of, me):
    count = lax.axis_size("dp")
    held = conv_store
    index = jnp.zeros((), jnp.int32)
    away = source_of[me] ^ me
    bit = count // 2
    place = 1
    while bit > 0:
        other = swap(held, "dp", bit)
        held = jnp.concatenate([held, other], axis=0)
        index = index + place * ((away // bit) & 1)
        bit //= 2
        place *= 2
    return lax.dynamic_index_in_dim(held, index, 0, keepdims=False)


def local(
    xbc,
    gate_z,
    dt_raw,
    conv_weight,
    conv_bias,
    dt_bias,
    decay_rate,
    d_skip,
    norm_gain,
    ssm_store,
    conv_store,
    source_of,
    prefix_len,
    span_len,
):
    me = lax.axis_index("dp")
    owners = lax.axis_size("dp")
    core = lax.axis_index("tensor").astype(jnp.int32).reshape(1)
    direct = owners <= DIRECT_MAX
    order = offsets(owners)
    state = ssm_store.reshape(owners, -1, STATE)
    rims = gather_rims(conv_store, source_of, me)
    if direct:
        held = [None] * owners
        far = [k for k in order if 2 * k >= owners]
        near = [k for k in order if 2 * k < owners]
        for some in (far, near + [0]):
            for k, piece in zip(some, cut_stage(state, some)):
                held[k] = swap(piece, "dp", k) if k else piece
    else:
        held = lax.all_to_all(state, "dp", split_axis=0, concat_axis=0, tiled=True)

    peer_xbc = swap(xbc, "tensor", 1)
    peer_gate = swap(gate_z, "tensor", 1)
    peer_dt = swap(dt_raw, "tensor", 1)
    heads = jnp.pad(jnp.stack([dt_bias, decay_rate]), ((0, 6), (0, LANES - dt_bias.shape[0])))
    intra, carry, c_proj = main_stage(
        core,
        prefix_len,
        d_skip,
        xbc,
        peer_xbc,
        conv_weight,
        conv_bias.reshape(1, -1),
        rims,
        gate_z,
        peer_gate,
        dt_raw,
        peer_dt,
        heads,
    )

    if direct:
        got = [None] * owners
        slots = order + [0]
        picked = pick_stage(me.astype(jnp.int32).reshape(1), source_of, held, slots)
        for k, piece in zip(slots, picked):
            got[k] = swap(piece, "dp", k) if k else piece
        turn = source_of[me] ^ me
    else:
        picked = jnp.take(held, source_of, axis=0)
        arrived = lax.all_to_all(picked, "dp", split_axis=0, concat_axis=0, tiled=True)
        got = [arrived.reshape(-1, STATE)]
        turn = jnp.zeros((), jnp.int32)
    return tail_stage(
        turn.astype(jnp.int32).reshape(1),
        span_len,
        got,
        intra,
        carry,
        c_proj,
        norm_gain.reshape(1, -1),
    )


def solution(mesh):
    in_specs = (
        P(("groups", "dp", "tensor"), None),
        P(("groups", "dp", "tensor"), None),
        P(("groups", "dp", "tensor"), None),
        P(),
        P(),
        P("tensor"),
        P("tensor"),
        P("tensor"),
        P("tensor"),
        P(("groups", "dp"), "tensor", None, None),
        P(("groups", "dp"), None, "tensor"),
        P("groups"),
        P(("groups", "dp")),
        P(("groups", "dp")),
    )
    out_specs = P(("groups", "dp"), "tensor")

    return jax.shard_map(local, mesh=mesh, in_specs=in_specs, out_specs=out_specs, check_vma=False)
```

```python
import functools

import jax
import jax.numpy as jnp
from jax import lax
from jax.experimental import pallas as pl
from jax.experimental.pallas import tpu as pltpu
from jax.sharding import PartitionSpec as P


HEAD_DIM = 64
STATE = 128
NORM_WIDTH = 2048
EPSILON = 1e-05
LANES = 128
DIRECT_MAX = 8


def swap(value, axis, offset):
    count = lax.axis_size(axis)
    return lax.ppermute(value, axis, [(i, i ^ offset) for i in range(count)])


def keep_in(space, *values):
    return [pltpu.with_memory_space_constraint(value, space) for value in values]


def offsets(count):
    return sorted(range(1, count), key=lambda k: (-(k.bit_length()), k))


def main_kernel(
    core_ref,
    live_ref,
    skip_ref,
    own_x,
    peer_x,
    own_bc,
    peer_bc,
    weight_x,
    weight_bc,
    bias_x,
    bias_bc,
    rims_x,
    rims_bc,
    own_gate,
    peer_gate,
    own_dt,
    peer_dt,
    head_rows,
    intra_out,
    carry_out,
    c_out,
    extended,
    scores,
    columns,
    cum_rows,
    step_rows,
):
    block = pl.program_id(0)
    count = 2 * own_x.shape[0]
    half = own_x.shape[0]
    width = own_x.shape[1]
    per_block = width // HEAD_DIM
    groups = c_out.shape[1] // STATE
    blocks = pl.num_programs(0)
    first = core_ref[0] == 0
    live = live_ref[0] > 0
    taps = weight_x.shape[0]
    pad = 8 - (taps - 1)

    def whole(own, peer):
        mine = own[...].astype(jnp.float32)
        other = peer[...].astype(jnp.float32)
        return jnp.where(first, mine, other), jnp.where(first, other, mine)

    def convolve(own, peer, rims, weight, bias):
        low, high = whole(own, peer)
        edge = rims[...].astype(jnp.float32)
        extended[pad:8, :] = jnp.where(live, edge, jnp.zeros_like(edge))
        extended[8 : 8 + half, :] = low
        extended[8 + half : 8 + count, :] = high
        total = jnp.broadcast_to(bias[...], (count, width))
        for k in range(taps):
            total = total + weight[k : k + 1, :] * extended[pad + k : pad + k + count, :]
        return jax.nn.silu(total).astype(jnp.bfloat16)

    row = lax.broadcasted_iota(jnp.int32, (count, LANES), 0)
    lane = lax.broadcasted_iota(jnp.int32, (count, LANES), 1)

    @pl.when(block == 0)
    def _():
        active = convolve(own_bc, peer_bc, rims_bc, weight_bc, bias_bc)
        c_out[...] = active[:, groups * STATE :]
        for g in range(groups):
            b = active[:, g * STATE : (g + 1) * STATE]
            c = active[:, (groups + g) * STATE : (groups + g + 1) * STATE]
            product = lax.dot_general(
                c, b, (((1,), (1,)), ((), ())), preferred_element_type=jnp.float32
            )
            scores[g] = jnp.where(row >= lane, product, 0.0)
        low, high = whole(own_dt, peer_dt)
        raw = jnp.concatenate([low, high], axis=0)
        raw = jnp.where(first, raw, pltpu.roll(raw, LANES // 2, 1))
        step = jax.nn.softplus(raw + head_rows[0:1, :])
        total = -head_rows[1:2, :] * step
        shift = 1
        while shift < count:
            total = total + jnp.where(row >= shift, pltpu.roll(total, shift, 0), 0.0)
            shift *= 2
        cum_rows[...] = total.T
        step_rows[...] = step.T
        for i in range(columns.shape[0]):
            columns[i] = total[:, i * per_block : (i + 1) * per_block]

    active = convolve(own_x, peer_x, rims_x, weight_x, bias_x)
    low, high = whole(own_gate, peer_gate)
    gate = jax.nn.silu(jnp.concatenate([low, high], axis=0))
    score = scores[block // (blocks // groups)]
    column = columns[block]
    at = pl.multiple_of(block * per_block, per_block)
    cum_row = cum_rows[pl.ds(at, per_block), :]
    step_row = step_rows[pl.ds(at, per_block), :]
    left = lane < HEAD_DIM
    scale = jnp.where(live, 1.0, 0.0)
    for pair in range(per_block // 2):
        spread, weights = [], []
        for j in (2 * pair, 2 * pair + 1):
            cum = jnp.broadcast_to(column[:, j : j + 1], (count, LANES))
            decay = jnp.exp(jnp.minimum(cum - cum_row[j : j + 1, :], 0.0))
            weights.append((decay * score * step_row[j : j + 1, :]).astype(jnp.bfloat16))
            spread.append(cum)
        lanes = slice(pair * LANES, (pair + 1) * LANES)
        x = active[:, lanes]
        zero = jnp.zeros_like(x)
        stacked = jnp.concatenate([jnp.where(left, x, zero), jnp.where(left, zero, x)], axis=0)
        intra = lax.dot_general(
            jnp.concatenate(weights, axis=1),
            stacked,
            (((1,), (0,)), ((), ())),
            preferred_element_type=jnp.float32,
        )
        skip = jnp.where(left, skip_ref[at + 2 * pair], skip_ref[at + 2 * pair + 1])
        gates = gate[:, lanes]
        intra_out[:, lanes] = (intra + skip * x.astype(jnp.float32)) * gates
        decayed = jnp.exp(jnp.where(left, spread[0], spread[1]))
        carry_out[:, lanes] = gates * decayed * scale


def main_stage(core, live, d_skip, xbc, peer_xbc, weight, bias, rims, gate, peer_gate, dt, peer_dt, heads):
    rows, channels = xbc.shape
    half = channels // 2
    count = 2 * rows
    inner = gate.shape[1] // 2
    width = half - inner
    groups = width // (2 * STATE)
    blocks = inner // width
    per_half = half // width
    per_inner = inner // width
    at_x = lambda i, core, *_: (0, core[0] * per_half + i)
    at_bc = lambda i, core, *_: (0, core[0] * per_half + blocks)
    at_gate = lambda i, core, *_: (0, core[0] * per_inner + i)
    fixed = lambda i, *_: (0, 0)
    step = lambda i, *_: (0, i)
    last = lambda i, *_: (0, blocks)
    taps = weight.shape[0]
    token = lambda index: pl.BlockSpec((rows, width), index)
    grid_spec = pltpu.PrefetchScalarGridSpec(
        num_scalar_prefetch=3,
        grid=(blocks,),
        in_specs=[
            token(at_x),
            token(at_x),
            token(at_bc),
            token(at_bc),
            pl.BlockSpec((taps, width), at_x),
            pl.BlockSpec((taps, width), at_bc),
            pl.BlockSpec((1, width), at_x),
            pl.BlockSpec((1, width), at_bc),
            pl.BlockSpec((taps - 1, width), step),
            pl.BlockSpec((taps - 1, width), last),
            token(at_gate),
            token(at_gate),
            pl.BlockSpec((rows, LANES), fixed),
            pl.BlockSpec((rows, LANES), fixed),
            pl.BlockSpec((8, LANES), fixed),
        ],
        out_specs=[
            pl.BlockSpec((count, width), step),
            pl.BlockSpec((count, width), step),
            pl.BlockSpec((count, groups * STATE), fixed),
        ],
        scratch_shapes=[
            pltpu.VMEM((count + 8, width), jnp.float32),
            pltpu.VMEM((groups, count, LANES), jnp.float32),
            pltpu.VMEM((blocks, count, width // HEAD_DIM), jnp.float32),
            pltpu.VMEM((LANES, count), jnp.float32),
            pltpu.VMEM((LANES, count), jnp.float32),
        ],
    )
    xbc, peer_xbc, gate, peer_gate = keep_in(pltpu.HBM, xbc, peer_xbc, gate, peer_gate)
    return pl.pallas_call(
        main_kernel,
        grid_spec=grid_spec,
        out_shape=[
            jax.ShapeDtypeStruct((count, inner), jnp.float32),
            jax.ShapeDtypeStruct((count, inner), jnp.float32),
            jax.ShapeDtypeStruct((count, groups * STATE), jnp.bfloat16),
        ],
        compiler_params=pltpu.CompilerParams(vmem_limit_bytes=16 << 20),
        cost_estimate=pl.CostEstimate(flops=400_000_000, bytes_accessed=8_000_000, transcendentals=2_000_000),
        name="main_stage",
    )(core, live, d_skip, xbc, peer_xbc, xbc, peer_xbc, weight, weight, bias, bias, rims, rims, gate, peer_gate, dt, peer_dt, heads)


def tail_kernel(base, has_before, turn_ref, span_ref, *refs):
    out, wide, narrow, sems = refs[-4:]
    intra, carry, c_proj, gain = refs[-8 - has_before : -4 - has_before]
    pieces = refs[: -8 - has_before]
    tokens = wide.shape[0]
    count, rows = len(pieces), pieces[0].shape[0]
    group = base ^ (turn_ref[0] // count)
    within = turn_ref[0] % count
    keep = lax.broadcasted_iota(jnp.int32, (tokens, 1), 0) < span_ref[0]
    c = c_proj[:, pl.ds(pl.multiple_of(group * STATE, STATE), STATE)]
    part = min(rows, 512)
    total = jnp.zeros((tokens, 1), jnp.float32)
    places = []
    for k, piece in enumerate(pieces):
        for at in range(0, rows, part):
            local_at = pl.multiple_of((k ^ within) * rows + at, part)
            column = pl.multiple_of(group * NORM_WIDTH + local_at, part)
            carried = lax.dot_general(
                c, piece[at : at + part, :], (((1,), (1,)), ((), ())), preferred_element_type=jnp.float32
            )
            value = intra[:, pl.ds(column, part)] + carry[:, pl.ds(column, part)] * carried
            total = total + jnp.sum(value * value, axis=1, keepdims=True)
            index = len(places)
            wide[:, index * part : (index + 1) * part] = value
            places.append(column)
    scale = jnp.where(keep, lax.rsqrt(total * (1.0 / NORM_WIDTH) + EPSILON), 0.0)
    copies = []
    for index, column in enumerate(places):
        lanes = slice(index * part, (index + 1) * part)
        normed = wide[:, lanes] * scale * gain[:, pl.ds(column, part)]
        narrow[:, lanes] = jnp.where(keep, normed, 0.0).astype(jnp.bfloat16)
        copy = pltpu.make_async_copy(narrow.at[:, lanes], out.at[:, pl.ds(column, part)], sems.at[index])
        copy.start()
        copies.append(copy)
    for copy in copies:
        copy.wait()


def tail_stage(base, turn, span_len, pieces, intra, carry, c_proj, gain, before=None):
    tokens, _ = intra.shape
    vmem = pl.BlockSpec(memory_space=pltpu.VMEM)
    whole = pl.BlockSpec(memory_space=pltpu.HBM)
    earlier = [] if before is None else [before]
    parts = NORM_WIDTH // min(pieces[0].shape[0], 512)
    grid_spec = pltpu.PrefetchScalarGridSpec(
        num_scalar_prefetch=2,
        grid=(),
        in_specs=[vmem] * (len(pieces) + 4) + [whole] * len(earlier),
        out_specs=whole,
        scratch_shapes=[
            pltpu.VMEM((tokens, NORM_WIDTH), jnp.float32),
            pltpu.VMEM((tokens, NORM_WIDTH), jnp.bfloat16),
            pltpu.SemaphoreType.DMA((parts,)),
        ],
    )
    return pl.pallas_call(
        functools.partial(tail_kernel, base, len(earlier)),
        grid_spec=grid_spec,
        out_shape=jax.ShapeDtypeStruct(intra.shape, jnp.bfloat16),
        input_output_aliases={2 + len(pieces) + 4: 0} if earlier else {},
        compiler_params=pltpu.CompilerParams(vmem_limit_bytes=16 << 20),
        cost_estimate=pl.CostEstimate(flops=70_000_000, bytes_accessed=3_000_000, transcendentals=0),
    )(turn, span_len, *pieces, intra, carry, c_proj, gain, *earlier)


def cut_kernel(chosen, state, *refs):
    pieces, sems = refs[: len(chosen)], refs[-1]
    copies = []
    for i, (k, piece) in enumerate(zip(chosen, pieces)):
        copy = pltpu.make_async_copy(state.at[k], piece, sems.at[i])
        copy.start()
        copies.append(copy)
    for copy in copies:
        copy.wait()


def cut_stage(state, chosen):
    return pl.pallas_call(
        functools.partial(cut_kernel, chosen),
        in_specs=[pl.BlockSpec(memory_space=pltpu.HBM)],
        out_specs=[pl.BlockSpec(memory_space=pltpu.VMEM)] * len(chosen),
        out_shape=[pltpu.VMEM(state.shape[1:], state.dtype)] * len(chosen),
        scratch_shapes=[pltpu.SemaphoreType.DMA((len(chosen),))],
        compiler_params=pltpu.CompilerParams(vmem_limit_bytes=8 << 20),
        name="cut_stage",
    )(*keep_in(pltpu.HBM, state))


def pick_kernel(order, me_ref, turned_ref, *refs):
    count = len(order)
    held, slots = refs[:count], refs[count:]
    for slot, k in zip(slots, order):
        wanted = turned_ref[me_ref[0] ^ k]
        for r in range(count):

            @pl.when(wanted == r)
            def _(slot=slot, r=r):
                slot[...] = held[r][...]


def pick_stage(me, turned, held, order):
    vmem = pl.BlockSpec(memory_space=pltpu.VMEM)
    grid_spec = pltpu.PrefetchScalarGridSpec(
        num_scalar_prefetch=2,
        grid=(),
        in_specs=[vmem] * len(held),
        out_specs=[vmem] * len(order),
    )
    shape = pltpu.VMEM(held[0].shape, held[0].dtype)
    return pl.pallas_call(
        functools.partial(pick_kernel, tuple(order)),
        grid_spec=grid_spec,
        out_shape=[shape] * len(order),
        compiler_params=pltpu.CompilerParams(vmem_limit_bytes=8 << 20),
        name="pick_stage",
    )(me, turned, *keep_in(pltpu.VMEM, *held))


def gather_rims(conv_store, source_of, me):
    count = lax.axis_size("dp")
    held = conv_store
    index = jnp.zeros((), jnp.int32)
    away = source_of[me] ^ me
    bit = count // 2
    place = 1
    while bit > 0:
        other = swap(held, "dp", bit)
        held = jnp.concatenate([held, other], axis=0)
        index = index + place * ((away // bit) & 1)
        bit //= 2
        place *= 2
    return lax.dynamic_index_in_dim(held, index, 0, keepdims=False)


def local(
    xbc,
    gate_z,
    dt_raw,
    conv_weight,
    conv_bias,
    dt_bias,
    decay_rate,
    d_skip,
    norm_gain,
    ssm_store,
    conv_store,
    source_of,
    prefix_len,
    span_len,
):
    me = lax.axis_index("dp")
    owners = lax.axis_size("dp")
    core = lax.axis_index("tensor").astype(jnp.int32).reshape(1)
    direct = owners <= DIRECT_MAX
    order = offsets(owners)
    state = ssm_store.reshape(owners, -1, STATE)
    rims = gather_rims(conv_store, source_of, me)
    if direct:
        held = [None] * owners
        every = order + [0]
        for k, piece in zip(every, cut_stage(state, every)):
            held[k] = swap(piece, "dp", k) if k else piece
    else:
        held = lax.all_to_all(state, "dp", split_axis=0, concat_axis=0, tiled=True)

    peer_xbc = swap(xbc, "tensor", 1)
    peer_gate = swap(gate_z, "tensor", 1)
    peer_dt = swap(dt_raw, "tensor", 1)
    heads = jnp.pad(jnp.stack([dt_bias, decay_rate]), ((0, 6), (0, LANES - dt_bias.shape[0])))
    intra, carry, c_proj = main_stage(
        core,
        prefix_len,
        d_skip,
        xbc,
        peer_xbc,
        conv_weight,
        conv_bias.reshape(1, -1),
        rims,
        gate_z,
        peer_gate,
        dt_raw,
        peer_dt,
        heads,
    )

    if direct:
        got = [None] * owners
        slots = order + [0]
        picked = pick_stage(me.astype(jnp.int32).reshape(1), source_of ^ me, held, slots)
        for k, piece in zip(slots, picked):
            got[k] = swap(piece, "dp", k) if k else piece
        turn = source_of[me] ^ me
    else:
        picked = jnp.take(held, source_of, axis=0)
        arrived = lax.all_to_all(picked, "dp", split_axis=0, concat_axis=0, tiled=True)
        got = list(arrived.reshape(-1, NORM_WIDTH, STATE))
        turn = jnp.zeros((), jnp.int32)
    turn = turn.astype(jnp.int32).reshape(1)
    gain = norm_gain.reshape(1, -1)
    mixed = None
    norms = norm_gain.shape[0] // NORM_WIDTH
    share = len(got) // norms
    for base in range(norms):
        mine = got[base * share : (base + 1) * share]
        mixed = tail_stage(base, turn, span_len, mine, intra, carry, c_proj, gain, mixed)
    return mixed


def solution(mesh):
    in_specs = (
        P(("groups", "dp", "tensor"), None),
        P(("groups", "dp", "tensor"), None),
        P(("groups", "dp", "tensor"), None),
        P(),
        P(),
        P("tensor"),
        P("tensor"),
        P("tensor"),
        P("tensor"),
        P(("groups", "dp"), "tensor", None, None),
        P(("groups", "dp"), None, "tensor"),
        P("groups"),
        P(("groups", "dp")),
        P(("groups", "dp")),
    )
    out_specs = P(("groups", "dp"), "tensor")

    return jax.shard_map(local, mesh=mesh, in_specs=in_specs, out_specs=out_specs, check_vma=False)
```

```python
import functools

import jax
import jax.numpy as jnp
from jax import lax
from jax.experimental import pallas as pl
from jax.experimental.pallas import tpu as pltpu
from jax.sharding import PartitionSpec as P


HEAD_DIM = 64
STATE = 128
NORM_WIDTH = 2048
EPSILON = 1e-05
LANES = 128
DIRECT_MAX = 8


def swap(value, axis, offset):
    count = lax.axis_size(axis)
    return lax.ppermute(value, axis, [(i, i ^ offset) for i in range(count)])


CORE, ME, PREFIX, SPAN, TURNED = 0, 1, 2, 3, 4


def silu(value):
    half = 0.5 * value
    return half + half * jnp.tanh(half)


def keep_in(space, *values):
    return [pltpu.with_memory_space_constraint(value, space) for value in values]


def offsets(count):
    return sorted(range(1, count), key=lambda k: (-(k.bit_length()), k))


def main_kernel(
    rims_count,
    plan,
    skip_ref,
    own_x,
    peer_x,
    own_bc,
    peer_bc,
    weight_x,
    weight_bc,
    bias_x,
    bias_bc,
    own_gate,
    peer_gate,
    own_dt,
    peer_dt,
    dt_bias,
    decay_rate,
    *refs,
):
    rims = refs[:rims_count]
    intra_out, carry_out, c_out, extended, gates, scores, columns, cum_rows, step_rows = refs[rims_count:]
    block = pl.program_id(0)
    half, width = own_x.shape
    count = 2 * half
    per_block = width // HEAD_DIM
    groups = c_out.shape[1] // STATE
    blocks = pl.num_programs(0)
    live = plan[PREFIX] > 0
    taps = weight_x.shape[0]
    pad = 8 - (taps - 1)
    mine = pl.multiple_of(plan[CORE] * half, half)
    theirs = pl.multiple_of(half - mine, half)

    def edges(at):
        lanes = pl.ds(pl.multiple_of(at * width, width), width)
        edge = rims[0][0, :, lanes]
        if rims_count > 1:
            away = plan[TURNED + plan[ME]]
            choice = jnp.where((away & 1) == 0, away // 2, rims_count - 1)
            for i in range(1, rims_count):
                edge = jnp.where(choice == i, rims[i][0, :, lanes], edge)
        edge = edge.astype(jnp.float32)
        return jnp.where(live, edge, jnp.zeros_like(edge))

    def convolve(own, peer, at, weight, bias):
        extended[pad:8, :] = edges(at)
        extended[pl.ds(8 + mine, half), :] = own[...].astype(jnp.float32)
        extended[pl.ds(8 + theirs, half), :] = peer[...].astype(jnp.float32)
        total = jnp.broadcast_to(bias[...], (count, width))
        for k in range(taps):
            total = total + weight[k : k + 1, :] * extended[pad + k : pad + k + count, :]
        return silu(total).astype(jnp.bfloat16)

    row = lax.broadcasted_iota(jnp.int32, (count, LANES), 0)
    lane = lax.broadcasted_iota(jnp.int32, (count, LANES), 1)

    @pl.when(block == 0)
    def _():
        active = convolve(own_bc, peer_bc, blocks, weight_bc, bias_bc)
        c_out[...] = active[:, groups * STATE :]
        for g in range(groups):
            b = active[:, g * STATE : (g + 1) * STATE]
            c = active[:, (groups + g) * STATE : (groups + g + 1) * STATE]
            product = lax.dot_general(
                c, b, (((1,), (1,)), ((), ())), preferred_element_type=jnp.float32
            )
            scores[g] = jnp.where(row >= lane, product, 0.0)
        extended[pl.ds(8 + mine, half), :LANES] = own_dt[...].astype(jnp.float32)
        extended[pl.ds(8 + theirs, half), :LANES] = peer_dt[...].astype(jnp.float32)
        raw = extended[8 : 8 + count, :LANES]
        raw = jnp.where(plan[CORE] == 0, raw, pltpu.roll(raw, LANES // 2, 1))
        spare = jnp.zeros((1, LANES - dt_bias.shape[1]), jnp.float32)
        step = jax.nn.softplus(raw + jnp.concatenate([dt_bias[...], spare], axis=1))
        total = -jnp.concatenate([decay_rate[...], spare], axis=1) * step
        shift = 1
        while shift < count:
            total = total + jnp.where(row >= shift, pltpu.roll(total, shift, 0), 0.0)
            shift *= 2
        cum_rows[...] = total.T
        step_rows[...] = step.T
        for i in range(columns.shape[0]):
            columns[i] = total[:, i * per_block : (i + 1) * per_block]

    active = convolve(own_x, peer_x, block, weight_x, bias_x)
    gates[pl.ds(mine, half), :] = silu(own_gate[...].astype(jnp.float32))
    gates[pl.ds(theirs, half), :] = silu(peer_gate[...].astype(jnp.float32))
    score = scores[block // (blocks // groups)]
    column = columns[block]
    at = pl.multiple_of(block * per_block, per_block)
    cum_row = cum_rows[pl.ds(at, per_block), :]
    step_row = step_rows[pl.ds(at, per_block), :]
    left = lane < HEAD_DIM
    scale = jnp.where(live, 1.0, 0.0)
    for pair in range(per_block // 2):
        spread, weights = [], []
        for j in (2 * pair, 2 * pair + 1):
            cum = jnp.broadcast_to(column[:, j : j + 1], (count, LANES))
            decay = jnp.exp(jnp.minimum(cum - cum_row[j : j + 1, :], 0.0))
            weights.append((decay * score * step_row[j : j + 1, :]).astype(jnp.bfloat16))
            spread.append(cum)
        lanes = slice(pair * LANES, (pair + 1) * LANES)
        x = active[:, lanes]
        zero = jnp.zeros_like(x)
        stacked = jnp.concatenate([jnp.where(left, x, zero), jnp.where(left, zero, x)], axis=0)
        intra = lax.dot_general(
            jnp.concatenate(weights, axis=1),
            stacked,
            (((1,), (0,)), ((), ())),
            preferred_element_type=jnp.float32,
        )
        skip = jnp.where(left, skip_ref[at + 2 * pair], skip_ref[at + 2 * pair + 1])
        gate = gates[:, lanes]
        intra_out[:, lanes] = (intra + skip * x.astype(jnp.float32)) * gate
        decayed = jnp.exp(jnp.where(left, spread[0], spread[1]))
        carry_out[:, lanes] = gate * decayed * scale


def main_stage(plan, d_skip, xbc, peer_xbc, weight, bias, gate, peer_gate, dt, peer_dt, dt_bias, decay_rate, rims):
    rows, channels = xbc.shape
    half = channels // 2
    count = 2 * rows
    inner = gate.shape[1] // 2
    width = half - inner
    groups = width // (2 * STATE)
    blocks = inner // width
    per_half = half // width
    per_inner = inner // width
    heads = dt_bias.shape[0]
    at_x = lambda i, plan, *_: (0, plan[CORE] * per_half + i)
    at_bc = lambda i, plan, *_: (0, plan[CORE] * per_half + blocks)
    at_gate = lambda i, plan, *_: (0, plan[CORE] * per_inner + i)
    fixed = lambda i, *_: (0, 0)
    step = lambda i, *_: (0, i)
    taps = weight.shape[0]
    token = lambda index: pl.BlockSpec((rows, width), index)
    grid_spec = pltpu.PrefetchScalarGridSpec(
        num_scalar_prefetch=2,
        grid=(blocks,),
        in_specs=[
            token(at_x),
            token(at_x),
            token(at_bc),
            token(at_bc),
            pl.BlockSpec((taps, width), at_x),
            pl.BlockSpec((taps, width), at_bc),
            pl.BlockSpec((1, width), at_x),
            pl.BlockSpec((1, width), at_bc),
            token(at_gate),
            token(at_gate),
            pl.BlockSpec((rows, LANES), fixed),
            pl.BlockSpec((rows, LANES), fixed),
            pl.BlockSpec((1, heads), fixed),
            pl.BlockSpec((1, heads), fixed),
        ]
        + [pl.BlockSpec((1, taps - 1, half), lambda i, *_: (0, 0, 0))] * len(rims),
        out_specs=[
            pl.BlockSpec((count, width), step),
            pl.BlockSpec((count, width), step),
            pl.BlockSpec((count, groups * STATE), fixed),
        ],
        scratch_shapes=[
            pltpu.VMEM((count + 8, width), jnp.float32),
            pltpu.VMEM((count, width), jnp.float32),
            pltpu.VMEM((groups, count, LANES), jnp.float32),
            pltpu.VMEM((blocks, count, width // HEAD_DIM), jnp.float32),
            pltpu.VMEM((LANES, count), jnp.float32),
            pltpu.VMEM((LANES, count), jnp.float32),
        ],
    )
    xbc, gate = keep_in(pltpu.HBM, xbc, gate)
    return pl.pallas_call(
        functools.partial(main_kernel, len(rims)),
        grid_spec=grid_spec,
        out_shape=[
            jax.ShapeDtypeStruct((count, inner), jnp.float32),
            jax.ShapeDtypeStruct((count, inner), jnp.float32),
            jax.ShapeDtypeStruct((count, groups * STATE), jnp.bfloat16),
        ],
        compiler_params=pltpu.CompilerParams(vmem_limit_bytes=16 << 20),
        cost_estimate=pl.CostEstimate(flops=400_000_000, bytes_accessed=8_000_000, transcendentals=2_000_000),
        name="main_stage",
    )(
        plan,
        d_skip,
        xbc,
        peer_xbc,
        xbc,
        peer_xbc,
        weight,
        weight,
        bias,
        bias,
        gate,
        peer_gate,
        dt,
        peer_dt,
        dt_bias.reshape(1, -1),
        decay_rate.reshape(1, -1),
        *rims,
    )


def tail_kernel(base, has_before, plan, *refs):
    out, wide, narrow, sems = refs[-4:]
    intra, carry, c_proj, gain = refs[-8 - has_before : -4 - has_before]
    pieces = refs[: -8 - has_before]
    tokens = wide.shape[0]
    count, rows = len(pieces), pieces[0].shape[0]
    turn = plan[TURNED + plan[ME]] if count > 1 else 0
    group = base ^ (turn // count)
    within = turn % count
    keep = lax.broadcasted_iota(jnp.int32, (tokens, 1), 0) < plan[SPAN]
    c = c_proj[:, pl.ds(pl.multiple_of(group * STATE, STATE), STATE)]
    part = min(rows, 512)
    total = jnp.zeros((tokens, 1), jnp.float32)
    places = []
    for k, piece in enumerate(pieces):
        for at in range(0, rows, part):
            local_at = pl.multiple_of((k ^ within) * rows + at, part)
            column = pl.multiple_of(group * NORM_WIDTH + local_at, part)
            carried = lax.dot_general(
                c, piece[at : at + part, :], (((1,), (1,)), ((), ())), preferred_element_type=jnp.float32
            )
            value = intra[:, pl.ds(column, part)] + carry[:, pl.ds(column, part)] * carried
            total = total + jnp.sum(value * value, axis=1, keepdims=True)
            index = len(places)
            wide[:, index * part : (index + 1) * part] = value
            places.append(column)
    scale = lax.rsqrt(total * (1.0 / NORM_WIDTH) + EPSILON)
    copies = []
    for index, column in enumerate(places):
        lanes = slice(index * part, (index + 1) * part)
        normed = wide[:, lanes] * scale * gain[:, pl.ds(column, part)]
        narrow[:, lanes] = jnp.where(keep, normed, 0.0).astype(jnp.bfloat16)
        copy = pltpu.make_async_copy(narrow.at[:, lanes], out.at[:, pl.ds(column, part)], sems.at[index])
        copy.start()
        copies.append(copy)
    for copy in copies:
        copy.wait()


def tail_stage(base, plan, pieces, intra, carry, c_proj, gain, before=None):
    tokens, _ = intra.shape
    vmem = pl.BlockSpec(memory_space=pltpu.VMEM)
    whole = pl.BlockSpec(memory_space=pltpu.HBM)
    earlier = [] if before is None else [before]
    parts = NORM_WIDTH // min(pieces[0].shape[0], 512)
    grid_spec = pltpu.PrefetchScalarGridSpec(
        num_scalar_prefetch=1,
        grid=(),
        in_specs=[vmem] * (len(pieces) + 4) + [whole] * len(earlier),
        out_specs=whole,
        scratch_shapes=[
            pltpu.VMEM((tokens, NORM_WIDTH), jnp.float32),
            pltpu.VMEM((tokens, NORM_WIDTH), jnp.bfloat16),
            pltpu.SemaphoreType.DMA((parts,)),
        ],
    )
    return pl.pallas_call(
        functools.partial(tail_kernel, base, len(earlier)),
        grid_spec=grid_spec,
        out_shape=jax.ShapeDtypeStruct(intra.shape, jnp.bfloat16),
        input_output_aliases={1 + len(pieces) + 4: 0} if earlier else {},
        compiler_params=pltpu.CompilerParams(vmem_limit_bytes=16 << 20),
        cost_estimate=pl.CostEstimate(flops=70_000_000, bytes_accessed=3_000_000, transcendentals=0),
    )(plan, *pieces, intra, carry, c_proj, gain, *earlier)


def plan_kernel(prefix_len, span_len, source_of, plan):
    me = lax.axis_index("dp")
    plan[CORE] = lax.axis_index("tensor")
    plan[ME] = me
    plan[PREFIX] = prefix_len[0]
    plan[SPAN] = span_len[0]
    for i in range(source_of.shape[0]):
        plan[TURNED + i] = source_of[i] ^ me


def plan_stage(prefix_len, span_len, source_of):
    smem = pl.BlockSpec(memory_space=pltpu.SMEM)
    return pl.pallas_call(
        plan_kernel,
        in_specs=[smem] * 3,
        out_specs=smem,
        out_shape=pltpu.SMEM((TURNED + source_of.shape[0],), jnp.int32),
        compiler_params=pltpu.CompilerParams(vmem_limit_bytes=1 << 20),
        name="plan_stage",
    )(prefix_len, span_len, source_of)


def cut_kernel(chosen, state, rims, *refs):
    pieces, rims_out, sems = refs[: len(chosen)], refs[-2], refs[-1]
    copies = []
    for i, (k, piece) in enumerate(zip(chosen, pieces)):
        copies.append(pltpu.make_async_copy(state.at[k], piece, sems.at[i]))
    copies.append(pltpu.make_async_copy(rims, rims_out, sems.at[len(chosen)]))
    for copy in copies:
        copy.start()
    for copy in copies:
        copy.wait()


def cut_stage(state, rims, chosen):
    return pl.pallas_call(
        functools.partial(cut_kernel, chosen),
        in_specs=[pl.BlockSpec(memory_space=pltpu.HBM)] * 2,
        out_specs=[pl.BlockSpec(memory_space=pltpu.VMEM)] * (len(chosen) + 1),
        out_shape=[pltpu.VMEM(state.shape[1:], state.dtype)] * len(chosen) + [pltpu.VMEM(rims.shape, rims.dtype)],
        scratch_shapes=[pltpu.SemaphoreType.DMA((len(chosen) + 1,))],
        compiler_params=pltpu.CompilerParams(vmem_limit_bytes=8 << 20),
        name="cut_stage",
    )(*keep_in(pltpu.HBM, state, rims))


def pick_kernel(order, column_count, plan, *refs):
    count = len(order)
    held, column = refs[:count], refs[count : count + column_count]
    slots, rim_out = refs[count + column_count : -1], refs[-1]
    for slot, k in zip(slots, order):
        wanted = plan[TURNED + (plan[ME] ^ k)]
        for r in range(count):

            @pl.when(wanted == r)
            def _(slot=slot, r=r):
                slot[...] = held[r][...]

    wanted = plan[TURNED + (plan[ME] ^ 1)] // 2
    for i in range(column_count):

        @pl.when(wanted == i)
        def _(i=i):
            rim_out[...] = column[i][...]


def pick_stage(plan, held, column, order):
    vmem = pl.BlockSpec(memory_space=pltpu.VMEM)
    grid_spec = pltpu.PrefetchScalarGridSpec(
        num_scalar_prefetch=1,
        grid=(),
        in_specs=[vmem] * (len(held) + len(column)),
        out_specs=[vmem] * (len(order) + 1),
    )
    shape = pltpu.VMEM(held[0].shape, held[0].dtype)
    return pl.pallas_call(
        functools.partial(pick_kernel, tuple(order), len(column)),
        grid_spec=grid_spec,
        out_shape=[shape] * len(order) + [pltpu.VMEM(column[0].shape, column[0].dtype)],
        compiler_params=pltpu.CompilerParams(vmem_limit_bytes=8 << 20),
        name="pick_stage",
    )(plan, *keep_in(pltpu.VMEM, *held), *keep_in(pltpu.VMEM, *column))


def column_rims(conv_store):
    count = lax.axis_size("dp")
    held = {0: conv_store}
    bit = count // 2
    while bit > 1:
        for k in sorted(held):
            held[k ^ bit] = swap(held[k], "dp", bit)
        bit //= 2
    return [held[2 * i] for i in range(count // 2)]


def gather_rims(conv_store, source_of, me):
    count = lax.axis_size("dp")
    held = conv_store
    index = jnp.zeros((), jnp.int32)
    away = source_of[me] ^ me
    bit = count // 2
    place = 1
    while bit > 0:
        held = jnp.concatenate([held, swap(held, "dp", bit)], axis=0)
        index = index + place * ((away // bit) & 1)
        bit //= 2
        place *= 2
    return lax.dynamic_index_in_dim(held, index, 0)


def local(
    xbc,
    gate_z,
    dt_raw,
    conv_weight,
    conv_bias,
    dt_bias,
    decay_rate,
    d_skip,
    norm_gain,
    ssm_store,
    conv_store,
    source_of,
    prefix_len,
    span_len,
):
    me = lax.axis_index("dp").astype(jnp.int32)
    owners = lax.axis_size("dp")
    direct = owners <= DIRECT_MAX
    order = offsets(owners)
    plan = plan_stage(prefix_len, span_len, source_of)
    state = ssm_store.reshape(owners, -1, STATE)
    if direct:
        held = [None] * owners
        every = order + [0]
        *pieces, own_rims = cut_stage(state, conv_store, every)
        column = column_rims(own_rims)
        for k, piece in zip(every, pieces):
            held[k] = swap(piece, "dp", k) if k else piece
        got = [None] * owners
        *picked, rim = pick_stage(plan, held, column, every)
        for k, piece in zip(every, picked):
            got[k] = swap(piece, "dp", k) if k else piece
        rims = column + [swap(rim, "dp", 1)]
    else:
        rims = [gather_rims(conv_store, source_of, me)]
        held = lax.all_to_all(state, "dp", split_axis=0, concat_axis=0, tiled=True)
        picked = jnp.take(held, source_of, axis=0)
        arrived = lax.all_to_all(picked, "dp", split_axis=0, concat_axis=0, tiled=True)
        got = list(arrived.reshape(-1, NORM_WIDTH, STATE))

    peer_xbc = swap(xbc, "tensor", 1)
    peer_gate = swap(gate_z, "tensor", 1)
    peer_dt = swap(dt_raw, "tensor", 1)
    intra, carry, c_proj = main_stage(
        plan,
        d_skip,
        xbc,
        peer_xbc,
        conv_weight,
        conv_bias.reshape(1, -1),
        gate_z,
        peer_gate,
        dt_raw,
        peer_dt,
        dt_bias,
        decay_rate,
        rims,
    )
    gain = norm_gain.reshape(1, -1)
    mixed = None
    norms = norm_gain.shape[0] // NORM_WIDTH
    share = len(got) // norms
    for base in range(norms):
        mine = got[base * share : (base + 1) * share]
        mixed = tail_stage(base, plan, mine, intra, carry, c_proj, gain, mixed)
    return mixed


def solution(mesh):
    in_specs = (
        P(("groups", "dp", "tensor"), None),
        P(("groups", "dp", "tensor"), None),
        P(("groups", "dp", "tensor"), None),
        P(),
        P(),
        P("tensor"),
        P("tensor"),
        P("tensor"),
        P("tensor"),
        P(("groups", "dp"), "tensor", None, None),
        P(("groups", "dp"), None, "tensor"),
        P("groups"),
        P(("groups", "dp")),
        P(("groups", "dp")),
    )
    out_specs = P(("groups", "dp"), "tensor")

    return jax.shard_map(local, mesh=mesh, in_specs=in_specs, out_specs=out_specs, check_vma=False)
```

```python
import functools

import jax
import jax.numpy as jnp
from jax import lax
from jax.experimental import pallas as pl
from jax.experimental.pallas import tpu as pltpu
from jax.sharding import PartitionSpec as P


HEAD_DIM = 64
STATE = 128
NORM_WIDTH = 2048
EPSILON = 1e-05
LANES = 128
DIRECT_MAX = 8


def swap(value, axis, offset):
    count = lax.axis_size(axis)
    return lax.ppermute(value, axis, [(i, i ^ offset) for i in range(count)])


CORE, ME, PREFIX, SPAN, TURNED = 0, 1, 2, 3, 4


def silu(value):
    half = 0.5 * value
    return half + half * jnp.tanh(half)


def keep_in(space, *values):
    return [pltpu.with_memory_space_constraint(value, space) for value in values]


def offsets(count):
    return sorted(range(1, count), key=lambda k: (-(k.bit_length()), k))


def main_kernel(
    rims_count,
    plan,
    skip_ref,
    own_x,
    peer_x,
    own_bc,
    peer_bc,
    weight_x,
    weight_bc,
    bias_x,
    bias_bc,
    own_gate,
    peer_gate,
    own_dt,
    peer_dt,
    dt_bias,
    decay_rate,
    *refs,
):
    rims = refs[:rims_count]
    intra_out, carry_out, c_out, extended, gates, scores, columns, cum_rows, step_rows = refs[rims_count:]
    block = pl.program_id(0)
    half, width = own_x.shape
    count = 2 * half
    per_block = width // HEAD_DIM
    groups = c_out.shape[1] // STATE
    blocks = pl.num_programs(0)
    live = plan[PREFIX] > 0
    taps = weight_x.shape[0]
    pad = 8 - (taps - 1)
    mine = pl.multiple_of(plan[CORE] * half, half)
    theirs = pl.multiple_of(half - mine, half)

    def edges(at):
        lanes = pl.ds(pl.multiple_of(at * width, width), width)
        edge = rims[0][0, :, lanes]
        if rims_count > 1:
            away = plan[TURNED + plan[ME]]
            choice = jnp.where((away & 1) == 0, away // 2, rims_count - 1)
            for i in range(1, rims_count):
                edge = jnp.where(choice == i, rims[i][0, :, lanes], edge)
        edge = edge.astype(jnp.float32)
        return jnp.where(live, edge, jnp.zeros_like(edge))

    def convolve(own, peer, at, weight, bias):
        extended[pad:8, :] = edges(at)
        extended[pl.ds(8 + mine, half), :] = own[...].astype(jnp.float32)
        extended[pl.ds(8 + theirs, half), :] = peer[...].astype(jnp.float32)
        total = jnp.broadcast_to(bias[...], (count, width))
        for k in range(taps):
            total = total + weight[k : k + 1, :] * extended[pad + k : pad + k + count, :]
        return silu(total).astype(jnp.bfloat16)

    row = lax.broadcasted_iota(jnp.int32, (count, LANES), 0)
    lane = lax.broadcasted_iota(jnp.int32, (count, LANES), 1)

    @pl.when(block == 0)
    def _():
        active = convolve(own_bc, peer_bc, blocks, weight_bc, bias_bc)
        c_out[...] = active[:, groups * STATE :]
        for g in range(groups):
            b = active[:, g * STATE : (g + 1) * STATE]
            c = active[:, (groups + g) * STATE : (groups + g + 1) * STATE]
            product = lax.dot_general(
                c, b, (((1,), (1,)), ((), ())), preferred_element_type=jnp.float32
            )
            scores[g] = jnp.where(row >= lane, product, 0.0)
        extended[pl.ds(8 + mine, half), :LANES] = own_dt[...].astype(jnp.float32)
        extended[pl.ds(8 + theirs, half), :LANES] = peer_dt[...].astype(jnp.float32)
        raw = extended[8 : 8 + count, :LANES]
        raw = jnp.where(plan[CORE] == 0, raw, pltpu.roll(raw, LANES // 2, 1))
        spare = jnp.zeros((1, LANES - dt_bias.shape[1]), jnp.float32)
        step = jax.nn.softplus(raw + jnp.concatenate([dt_bias[...], spare], axis=1))
        total = -jnp.concatenate([decay_rate[...], spare], axis=1) * step
        shift = 1
        while shift < count:
            total = total + jnp.where(row >= shift, pltpu.roll(total, shift, 0), 0.0)
            shift *= 2
        cum_rows[...] = total.T
        step_rows[...] = step.T
        for i in range(columns.shape[0]):
            columns[i] = total[:, i * per_block : (i + 1) * per_block]

    active = convolve(own_x, peer_x, block, weight_x, bias_x)
    gates[pl.ds(mine, half), :] = silu(own_gate[...].astype(jnp.float32))
    gates[pl.ds(theirs, half), :] = silu(peer_gate[...].astype(jnp.float32))
    score = scores[block // (blocks // groups)]
    column = columns[block]
    at = pl.multiple_of(block * per_block, per_block)
    cum_row = cum_rows[pl.ds(at, per_block), :]
    step_row = step_rows[pl.ds(at, per_block), :]
    left = lane < HEAD_DIM
    scale = jnp.where(live, 1.0, 0.0)
    for pair in range(per_block // 2):
        spread, weights = [], []
        for j in (2 * pair, 2 * pair + 1):
            cum = jnp.broadcast_to(column[:, j : j + 1], (count, LANES))
            decay = jnp.exp(jnp.minimum(cum - cum_row[j : j + 1, :], 0.0))
            weights.append((decay * score * step_row[j : j + 1, :]).astype(jnp.bfloat16))
            spread.append(cum)
        lanes = slice(pair * LANES, (pair + 1) * LANES)
        x = active[:, lanes]
        zero = jnp.zeros_like(x)
        stacked = jnp.concatenate([jnp.where(left, x, zero), jnp.where(left, zero, x)], axis=0)
        intra = lax.dot_general(
            jnp.concatenate(weights, axis=1),
            stacked,
            (((1,), (0,)), ((), ())),
            preferred_element_type=jnp.float32,
        )
        skip = jnp.where(left, skip_ref[at + 2 * pair], skip_ref[at + 2 * pair + 1])
        gate = gates[:, lanes]
        intra_out[:, lanes] = (intra + skip * x.astype(jnp.float32)) * gate
        decayed = jnp.exp(jnp.where(left, spread[0], spread[1]))
        carry_out[:, lanes] = gate * decayed * scale


def main_stage(plan, d_skip, xbc, peer_xbc, weight, bias, gate, peer_gate, dt, peer_dt, dt_bias, decay_rate, rims):
    rows, channels = xbc.shape
    half = channels // 2
    count = 2 * rows
    inner = gate.shape[1] // 2
    width = half - inner
    groups = width // (2 * STATE)
    blocks = inner // width
    per_half = half // width
    per_inner = inner // width
    heads = dt_bias.shape[0]
    at_x = lambda i, plan, *_: (0, plan[CORE] * per_half + i)
    at_bc = lambda i, plan, *_: (0, plan[CORE] * per_half + blocks)
    at_gate = lambda i, plan, *_: (0, plan[CORE] * per_inner + i)
    fixed = lambda i, *_: (0, 0)
    step = lambda i, *_: (0, i)
    taps = weight.shape[0]
    token = lambda index: pl.BlockSpec((rows, width), index)
    grid_spec = pltpu.PrefetchScalarGridSpec(
        num_scalar_prefetch=2,
        grid=(blocks,),
        in_specs=[
            token(at_x),
            token(at_x),
            token(at_bc),
            token(at_bc),
            pl.BlockSpec((taps, width), at_x),
            pl.BlockSpec((taps, width), at_bc),
            pl.BlockSpec((1, width), at_x),
            pl.BlockSpec((1, width), at_bc),
            token(at_gate),
            token(at_gate),
            pl.BlockSpec((rows, LANES), fixed),
            pl.BlockSpec((rows, LANES), fixed),
            pl.BlockSpec((1, heads), fixed),
            pl.BlockSpec((1, heads), fixed),
        ]
        + [pl.BlockSpec((1, taps - 1, half), lambda i, *_: (0, 0, 0))] * len(rims),
        out_specs=[
            pl.BlockSpec((count, width), step),
            pl.BlockSpec((count, width), step),
            pl.BlockSpec((count, groups * STATE), fixed),
        ],
        scratch_shapes=[
            pltpu.VMEM((count + 8, width), jnp.float32),
            pltpu.VMEM((count, width), jnp.float32),
            pltpu.VMEM((groups, count, LANES), jnp.float32),
            pltpu.VMEM((blocks, count, width // HEAD_DIM), jnp.float32),
            pltpu.VMEM((LANES, count), jnp.float32),
            pltpu.VMEM((LANES, count), jnp.float32),
        ],
    )
    xbc, gate = keep_in(pltpu.HBM, xbc, gate)
    return pl.pallas_call(
        functools.partial(main_kernel, len(rims)),
        grid_spec=grid_spec,
        out_shape=[
            jax.ShapeDtypeStruct((count, inner), jnp.float32),
            jax.ShapeDtypeStruct((count, inner), jnp.float32),
            jax.ShapeDtypeStruct((count, groups * STATE), jnp.bfloat16),
        ],
        compiler_params=pltpu.CompilerParams(vmem_limit_bytes=16 << 20),
        cost_estimate=pl.CostEstimate(flops=400_000_000, bytes_accessed=8_000_000, transcendentals=2_000_000),
        name="main_stage",
    )(
        plan,
        d_skip,
        xbc,
        peer_xbc,
        xbc,
        peer_xbc,
        weight,
        weight,
        bias,
        bias,
        gate,
        peer_gate,
        dt,
        peer_dt,
        dt_bias.reshape(1, -1),
        decay_rate.reshape(1, -1),
        *rims,
    )


def tail_kernel(base, has_before, plan, *refs):
    out, wide, narrow, sems = refs[-4:]
    intra, carry, c_proj, gain = refs[-8 - has_before : -4 - has_before]
    pieces = refs[: -8 - has_before]
    tokens = wide.shape[0]
    count, rows = len(pieces), pieces[0].shape[0]
    turn = plan[TURNED + plan[ME]] if count > 1 else 0
    group = base ^ (turn // count)
    within = turn % count
    keep = lax.broadcasted_iota(jnp.int32, (tokens, 1), 0) < plan[SPAN]
    c = c_proj[:, pl.ds(pl.multiple_of(group * STATE, STATE), STATE)]
    part = min(rows, 512)
    total = jnp.zeros((tokens, 1), jnp.float32)
    places = []
    for k, piece in enumerate(pieces):
        for at in range(0, rows, part):
            local_at = pl.multiple_of((k ^ within) * rows + at, part)
            column = pl.multiple_of(group * NORM_WIDTH + local_at, part)
            carried = lax.dot_general(
                c, piece[at : at + part, :], (((1,), (1,)), ((), ())), preferred_element_type=jnp.float32
            )
            value = intra[:, pl.ds(column, part)] + carry[:, pl.ds(column, part)] * carried
            total = total + jnp.sum(value * value, axis=1, keepdims=True)
            index = len(places)
            wide[:, index * part : (index + 1) * part] = value
            places.append(column)
    scale = lax.rsqrt(total * (1.0 / NORM_WIDTH) + EPSILON)
    copies = []
    for index, column in enumerate(places):
        lanes = slice(index * part, (index + 1) * part)
        normed = wide[:, lanes] * scale * gain[:, pl.ds(column, part)]
        narrow[:, lanes] = jnp.where(keep, normed, 0.0).astype(jnp.bfloat16)
        copy = pltpu.make_async_copy(narrow.at[:, lanes], out.at[:, pl.ds(column, part)], sems.at[index])
        copy.start()
        copies.append(copy)
    for copy in copies:
        copy.wait()


def tail_stage(base, plan, pieces, intra, carry, c_proj, gain, before=None):
    tokens, _ = intra.shape
    vmem = pl.BlockSpec(memory_space=pltpu.VMEM)
    whole = pl.BlockSpec(memory_space=pltpu.HBM)
    earlier = [] if before is None else [before]
    parts = NORM_WIDTH // min(pieces[0].shape[0], 512)
    grid_spec = pltpu.PrefetchScalarGridSpec(
        num_scalar_prefetch=1,
        grid=(),
        in_specs=[vmem] * (len(pieces) + 4) + [whole] * len(earlier),
        out_specs=whole,
        scratch_shapes=[
            pltpu.VMEM((tokens, NORM_WIDTH), jnp.float32),
            pltpu.VMEM((tokens, NORM_WIDTH), jnp.bfloat16),
            pltpu.SemaphoreType.DMA((parts,)),
        ],
    )
    return pl.pallas_call(
        functools.partial(tail_kernel, base, len(earlier)),
        grid_spec=grid_spec,
        out_shape=jax.ShapeDtypeStruct(intra.shape, jnp.bfloat16),
        input_output_aliases={1 + len(pieces) + 4: 0} if earlier else {},
        compiler_params=pltpu.CompilerParams(vmem_limit_bytes=16 << 20),
        cost_estimate=pl.CostEstimate(flops=70_000_000, bytes_accessed=3_000_000, transcendentals=0),
    )(plan, *pieces, intra, carry, c_proj, gain, *earlier)


def plan_kernel(prefix_len, span_len, source_of, plan):
    me = lax.axis_index("dp")
    plan[CORE] = lax.axis_index("tensor")
    plan[ME] = me
    plan[PREFIX] = prefix_len[0]
    plan[SPAN] = span_len[0]
    for i in range(source_of.shape[0]):
        plan[TURNED + i] = source_of[i] ^ me


def plan_stage(prefix_len, span_len, source_of):
    smem = pl.BlockSpec(memory_space=pltpu.SMEM)
    return pl.pallas_call(
        plan_kernel,
        in_specs=[smem] * 3,
        out_specs=smem,
        out_shape=pltpu.SMEM((TURNED + source_of.shape[0],), jnp.int32),
        compiler_params=pltpu.CompilerParams(vmem_limit_bytes=1 << 20),
        name="plan_stage",
    )(prefix_len, span_len, source_of)


def cut_kernel(chosen, state, rims, *refs):
    pieces, rims_out, sems = refs[: len(chosen)], refs[-2], refs[-1]
    copies = []
    for i, (k, piece) in enumerate(zip(chosen, pieces)):
        copies.append(pltpu.make_async_copy(state.at[k], piece, sems.at[i]))
    copies.append(pltpu.make_async_copy(rims, rims_out, sems.at[len(chosen)]))
    for copy in copies:
        copy.start()
    for copy in copies:
        copy.wait()


def cut_stage(state, rims, chosen):
    return pl.pallas_call(
        functools.partial(cut_kernel, chosen),
        in_specs=[pl.BlockSpec(memory_space=pltpu.HBM)] * 2,
        out_specs=[pl.BlockSpec(memory_space=pltpu.VMEM)] * (len(chosen) + 1),
        out_shape=[pltpu.VMEM(state.shape[1:], state.dtype)] * len(chosen) + [pltpu.VMEM(rims.shape, rims.dtype)],
        scratch_shapes=[pltpu.SemaphoreType.DMA((len(chosen) + 1,))],
        compiler_params=pltpu.CompilerParams(vmem_limit_bytes=8 << 20),
        name="cut_stage",
    )(*keep_in(pltpu.HBM, state, rims))


def pick_kernel(order, column_count, plan, *refs):
    count = len(order)
    held, column = refs[:count], refs[count : count + column_count]
    slots, rim_out = refs[count + column_count : -1], refs[-1]
    for slot, k in zip(slots, order):
        wanted = plan[TURNED + (plan[ME] ^ k)]
        for r in range(count):

            @pl.when(wanted == r)
            def _(slot=slot, r=r):
                slot[...] = held[r][...]

    wanted = plan[TURNED + (plan[ME] ^ 1)] // 2
    for i in range(column_count):

        @pl.when(wanted == i)
        def _(i=i):
            rim_out[...] = column[i][...]


def pick_stage(plan, held, column, order):
    vmem = pl.BlockSpec(memory_space=pltpu.VMEM)
    grid_spec = pltpu.PrefetchScalarGridSpec(
        num_scalar_prefetch=1,
        grid=(),
        in_specs=[vmem] * (len(held) + len(column)),
        out_specs=[vmem] * (len(order) + 1),
    )
    shape = pltpu.VMEM(held[0].shape, held[0].dtype)
    return pl.pallas_call(
        functools.partial(pick_kernel, tuple(order), len(column)),
        grid_spec=grid_spec,
        out_shape=[shape] * len(order) + [pltpu.VMEM(column[0].shape, column[0].dtype)],
        compiler_params=pltpu.CompilerParams(vmem_limit_bytes=8 << 20),
        name="pick_stage",
    )(plan, *keep_in(pltpu.VMEM, *held), *keep_in(pltpu.VMEM, *column))


def column_rims(conv_store, own_rims):
    count = lax.axis_size("dp")
    held = {0: conv_store}
    bit = count // 2
    while bit > 1:
        for k in sorted(held):
            held[k ^ bit] = swap(held[k], "dp", bit)
        held[0] = own_rims
        bit //= 2
    return [held[2 * i] for i in range(count // 2)]


def gather_rims(conv_store, source_of, me):
    count = lax.axis_size("dp")
    held = conv_store
    index = jnp.zeros((), jnp.int32)
    away = source_of[me] ^ me
    bit = count // 2
    place = 1
    while bit > 0:
        held = jnp.concatenate([held, swap(held, "dp", bit)], axis=0)
        index = index + place * ((away // bit) & 1)
        bit //= 2
        place *= 2
    return lax.dynamic_index_in_dim(held, index, 0)


def local(
    xbc,
    gate_z,
    dt_raw,
    conv_weight,
    conv_bias,
    dt_bias,
    decay_rate,
    d_skip,
    norm_gain,
    ssm_store,
    conv_store,
    source_of,
    prefix_len,
    span_len,
):
    me = lax.axis_index("dp").astype(jnp.int32)
    owners = lax.axis_size("dp")
    direct = owners <= DIRECT_MAX
    order = offsets(owners)
    plan = plan_stage(prefix_len, span_len, source_of)
    state = ssm_store.reshape(owners, -1, STATE)
    if direct:
        held = [None] * owners
        every = order + [0]
        *pieces, own_rims = cut_stage(state, conv_store, every[1:])
        column = column_rims(conv_store, own_rims)
        for k, piece in zip(every, [state[every[0]]] + pieces):
            held[k] = swap(piece, "dp", k) if k else piece
        got = [None] * owners
        *picked, rim = pick_stage(plan, held, column, every)
        for k, piece in zip(every, picked):
            got[k] = swap(piece, "dp", k) if k else piece
        rims = column + [swap(rim, "dp", 1)]
    else:
        rims = [gather_rims(conv_store, source_of, me)]
        held = lax.all_to_all(state, "dp", split_axis=0, concat_axis=0, tiled=True)
        picked = jnp.take(held, source_of, axis=0)
        arrived = lax.all_to_all(picked, "dp", split_axis=0, concat_axis=0, tiled=True)
        got = list(arrived.reshape(-1, NORM_WIDTH, STATE))

    peer_xbc = swap(xbc, "tensor", 1)
    peer_gate = swap(gate_z, "tensor", 1)
    peer_dt = swap(dt_raw, "tensor", 1)
    intra, carry, c_proj = main_stage(
        plan,
        d_skip,
        xbc,
        peer_xbc,
        conv_weight,
        conv_bias.reshape(1, -1),
        gate_z,
        peer_gate,
        dt_raw,
        peer_dt,
        dt_bias,
        decay_rate,
        rims,
    )
    gain = norm_gain.reshape(1, -1)
    mixed = None
    norms = norm_gain.shape[0] // NORM_WIDTH
    share = len(got) // norms
    for base in range(norms):
        mine = got[base * share : (base + 1) * share]
        mixed = tail_stage(base, plan, mine, intra, carry, c_proj, gain, mixed)
    return mixed


def solution(mesh):
    in_specs = (
        P(("groups", "dp", "tensor"), None),
        P(("groups", "dp", "tensor"), None),
        P(("groups", "dp", "tensor"), None),
        P(),
        P(),
        P("tensor"),
        P("tensor"),
        P("tensor"),
        P("tensor"),
        P(("groups", "dp"), "tensor", None, None),
        P(("groups", "dp"), None, "tensor"),
        P("groups"),
        P(("groups", "dp")),
        P(("groups", "dp")),
    )
    out_specs = P(("groups", "dp"), "tensor")

    return jax.shard_map(local, mesh=mesh, in_specs=in_specs, out_specs=out_specs, check_vma=False)
```

```python
import functools

import jax
import jax.numpy as jnp
from jax import lax
from jax.experimental import pallas as pl
from jax.experimental.pallas import tpu as pltpu
from jax.sharding import PartitionSpec as P


HEAD_DIM = 64
STATE = 128
NORM_WIDTH = 2048
EPSILON = 1e-05
LANES = 128
DIRECT_MAX = 8


def swap(value, axis, offset):
    count = lax.axis_size(axis)
    return lax.ppermute(value, axis, [(i, i ^ offset) for i in range(count)])


CORE, ME, PREFIX, SPAN, TURNED = 0, 1, 2, 3, 4


def silu(value):
    half = 0.5 * value
    return half + half * jnp.tanh(half)


def keep_in(space, *values):
    return [pltpu.with_memory_space_constraint(value, space) for value in values]


def offsets(count):
    return sorted(range(1, count), key=lambda k: (-(k.bit_length()), k))


def main_kernel(
    rims_count,
    plan,
    skip_ref,
    own_x,
    peer_x,
    own_bc,
    peer_bc,
    weight_x,
    weight_bc,
    bias_x,
    bias_bc,
    own_gate,
    peer_gate,
    own_dt,
    peer_dt,
    dt_bias,
    decay_rate,
    *refs,
):
    rims = refs[:rims_count]
    intra_out, carry_out, c_out, extended, gates, scores, columns, cum_rows, step_rows = refs[rims_count:]
    block = pl.program_id(0)
    half, width = own_x.shape
    count = 2 * half
    per_block = width // HEAD_DIM
    groups = c_out.shape[1] // STATE
    blocks = pl.num_programs(0)
    live = plan[PREFIX] > 0
    taps = weight_x.shape[0]
    pad = 8 - (taps - 1)
    mine = pl.multiple_of(plan[CORE] * half, half)
    theirs = pl.multiple_of(half - mine, half)

    def edges(at):
        lanes = pl.ds(pl.multiple_of(at * width, width), width)
        edge = rims[0][0, :, lanes]
        if rims_count > 1:
            away = plan[TURNED + plan[ME]]
            choice = jnp.where((away & 1) == 0, away // 2, rims_count - 1)
            for i in range(1, rims_count):
                edge = jnp.where(choice == i, rims[i][0, :, lanes], edge)
        edge = edge.astype(jnp.float32)
        return jnp.where(live, edge, jnp.zeros_like(edge))

    def convolve(own, peer, at, weight, bias):
        extended[pad:8, :] = edges(at)
        extended[pl.ds(8 + mine, half), :] = own[...].astype(jnp.float32)
        extended[pl.ds(8 + theirs, half), :] = peer[...].astype(jnp.float32)
        total = jnp.broadcast_to(bias[...], (count, width))
        for k in range(taps):
            total = total + weight[k : k + 1, :] * extended[pad + k : pad + k + count, :]
        return silu(total).astype(jnp.bfloat16)

    row = lax.broadcasted_iota(jnp.int32, (count, LANES), 0)
    lane = lax.broadcasted_iota(jnp.int32, (count, LANES), 1)

    @pl.when(block == 0)
    def _():
        active = convolve(own_bc, peer_bc, blocks, weight_bc, bias_bc)
        c_out[...] = active[:, groups * STATE :]
        for g in range(groups):
            b = active[:, g * STATE : (g + 1) * STATE]
            c = active[:, (groups + g) * STATE : (groups + g + 1) * STATE]
            product = lax.dot_general(
                c, b, (((1,), (1,)), ((), ())), preferred_element_type=jnp.float32
            )
            scores[g] = jnp.where(row >= lane, product, 0.0)
        extended[pl.ds(8 + mine, half), :LANES] = own_dt[...].astype(jnp.float32)
        extended[pl.ds(8 + theirs, half), :LANES] = peer_dt[...].astype(jnp.float32)
        raw = extended[8 : 8 + count, :LANES]
        raw = jnp.where(plan[CORE] == 0, raw, pltpu.roll(raw, LANES // 2, 1))
        spare = jnp.zeros((1, LANES - dt_bias.shape[1]), jnp.float32)
        step = jax.nn.softplus(raw + jnp.concatenate([dt_bias[...], spare], axis=1))
        total = -jnp.concatenate([decay_rate[...], spare], axis=1) * step
        shift = 1
        while shift < count:
            total = total + jnp.where(row >= shift, pltpu.roll(total, shift, 0), 0.0)
            shift *= 2
        cum_rows[...] = total.T
        step_rows[...] = step.T
        for i in range(columns.shape[0]):
            columns[i] = total[:, i * per_block : (i + 1) * per_block]

    active = convolve(own_x, peer_x, block, weight_x, bias_x)
    gates[pl.ds(mine, half), :] = silu(own_gate[...].astype(jnp.float32))
    gates[pl.ds(theirs, half), :] = silu(peer_gate[...].astype(jnp.float32))
    score = scores[block // (blocks // groups)]
    column = columns[block]
    at = pl.multiple_of(block * per_block, per_block)
    cum_row = cum_rows[pl.ds(at, per_block), :]
    step_row = step_rows[pl.ds(at, per_block), :]
    left = lane < HEAD_DIM
    scale = jnp.where(live, 1.0, 0.0)
    for pair in range(per_block // 2):
        spread, weights = [], []
        for j in (2 * pair, 2 * pair + 1):
            cum = jnp.broadcast_to(column[:, j : j + 1], (count, LANES))
            decay = jnp.exp(jnp.minimum(cum - cum_row[j : j + 1, :], 0.0))
            weights.append((decay * score * step_row[j : j + 1, :]).astype(jnp.bfloat16))
            spread.append(cum)
        lanes = slice(pair * LANES, (pair + 1) * LANES)
        x = active[:, lanes]
        zero = jnp.zeros_like(x)
        stacked = jnp.concatenate([jnp.where(left, x, zero), jnp.where(left, zero, x)], axis=0)
        intra = lax.dot_general(
            jnp.concatenate(weights, axis=1),
            stacked,
            (((1,), (0,)), ((), ())),
            preferred_element_type=jnp.float32,
        )
        skip = jnp.where(left, skip_ref[at + 2 * pair], skip_ref[at + 2 * pair + 1])
        gate = gates[:, lanes]
        intra_out[:, lanes] = (intra + skip * x.astype(jnp.float32)) * gate
        decayed = jnp.exp(jnp.where(left, spread[0], spread[1]))
        carry_out[:, lanes] = gate * decayed * scale


def main_stage(plan, d_skip, xbc, peer_xbc, weight, bias, gate, peer_gate, dt, peer_dt, dt_bias, decay_rate, rims):
    rows, channels = xbc.shape
    half = channels // 2
    count = 2 * rows
    inner = gate.shape[1] // 2
    width = half - inner
    groups = width // (2 * STATE)
    blocks = inner // width
    per_half = half // width
    per_inner = inner // width
    heads = dt_bias.shape[0]
    at_x = lambda i, plan, *_: (0, plan[CORE] * per_half + i)
    at_bc = lambda i, plan, *_: (0, plan[CORE] * per_half + blocks)
    at_gate = lambda i, plan, *_: (0, plan[CORE] * per_inner + i)
    fixed = lambda i, *_: (0, 0)
    step = lambda i, *_: (0, i)
    taps = weight.shape[0]
    token = lambda index: pl.BlockSpec((rows, width), index)
    grid_spec = pltpu.PrefetchScalarGridSpec(
        num_scalar_prefetch=2,
        grid=(blocks,),
        in_specs=[
            token(at_x),
            token(at_x),
            token(at_bc),
            token(at_bc),
            pl.BlockSpec((taps, width), at_x),
            pl.BlockSpec((taps, width), at_bc),
            pl.BlockSpec((1, width), at_x),
            pl.BlockSpec((1, width), at_bc),
            token(at_gate),
            token(at_gate),
            pl.BlockSpec((rows, LANES), fixed),
            pl.BlockSpec((rows, LANES), fixed),
            pl.BlockSpec((1, heads), fixed),
            pl.BlockSpec((1, heads), fixed),
        ]
        + [pl.BlockSpec((1, taps - 1, half), lambda i, *_: (0, 0, 0))] * len(rims),
        out_specs=[
            pl.BlockSpec((count, width), step),
            pl.BlockSpec((count, width), step),
            pl.BlockSpec((count, groups * STATE), fixed),
        ],
        scratch_shapes=[
            pltpu.VMEM((count + 8, width), jnp.float32),
            pltpu.VMEM((count, width), jnp.float32),
            pltpu.VMEM((groups, count, LANES), jnp.float32),
            pltpu.VMEM((blocks, count, width // HEAD_DIM), jnp.float32),
            pltpu.VMEM((LANES, count), jnp.float32),
            pltpu.VMEM((LANES, count), jnp.float32),
        ],
    )
    xbc, gate = keep_in(pltpu.HBM, xbc, gate)
    return pl.pallas_call(
        functools.partial(main_kernel, len(rims)),
        grid_spec=grid_spec,
        out_shape=[
            jax.ShapeDtypeStruct((count, inner), jnp.float32),
            jax.ShapeDtypeStruct((count, inner), jnp.float32),
            jax.ShapeDtypeStruct((count, groups * STATE), jnp.bfloat16),
        ],
        compiler_params=pltpu.CompilerParams(vmem_limit_bytes=16 << 20),
        cost_estimate=pl.CostEstimate(flops=400_000_000, bytes_accessed=8_000_000, transcendentals=2_000_000),
        name="main_stage",
    )(
        plan,
        d_skip,
        xbc,
        peer_xbc,
        xbc,
        peer_xbc,
        weight,
        weight,
        bias,
        bias,
        gate,
        peer_gate,
        dt,
        peer_dt,
        dt_bias.reshape(1, -1),
        decay_rate.reshape(1, -1),
        *rims,
    )


def tail_kernel(base, has_before, plan, *refs):
    out, wide, narrow, sems = refs[-4:]
    intra, carry, c_proj, gain = refs[-8 - has_before : -4 - has_before]
    pieces = refs[: -8 - has_before]
    tokens = wide.shape[0]
    count, rows = len(pieces), pieces[0].shape[0]
    turn = plan[TURNED + plan[ME]] if count > 1 else 0
    group = base ^ (turn // count)
    within = turn % count
    keep = lax.broadcasted_iota(jnp.int32, (tokens, 1), 0) < plan[SPAN]
    c = c_proj[:, pl.ds(pl.multiple_of(group * STATE, STATE), STATE)]
    part = min(rows, 512)
    total = jnp.zeros((tokens, 1), jnp.float32)
    places = []
    for k, piece in enumerate(pieces):
        for at in range(0, rows, part):
            local_at = pl.multiple_of((k ^ within) * rows + at, part)
            column = pl.multiple_of(group * NORM_WIDTH + local_at, part)
            carried = lax.dot_general(
                c, piece[at : at + part, :], (((1,), (1,)), ((), ())), preferred_element_type=jnp.float32
            )
            value = intra[:, pl.ds(column, part)] + carry[:, pl.ds(column, part)] * carried
            total = total + jnp.sum(value * value, axis=1, keepdims=True)
            index = len(places)
            wide[:, index * part : (index + 1) * part] = value
            places.append(column)
    scale = lax.rsqrt(total * (1.0 / NORM_WIDTH) + EPSILON)
    copies = []
    for index, column in enumerate(places):
        lanes = slice(index * part, (index + 1) * part)
        normed = wide[:, lanes] * scale * gain[:, pl.ds(column, part)]
        narrow[:, lanes] = jnp.where(keep, normed, 0.0).astype(jnp.bfloat16)
        copy = pltpu.make_async_copy(narrow.at[:, lanes], out.at[:, pl.ds(column, part)], sems.at[index])
        copy.start()
        copies.append(copy)
    for copy in copies:
        copy.wait()


def tail_stage(base, plan, pieces, intra, carry, c_proj, gain, before=None):
    tokens, _ = intra.shape
    vmem = pl.BlockSpec(memory_space=pltpu.VMEM)
    whole = pl.BlockSpec(memory_space=pltpu.HBM)
    earlier = [] if before is None else [before]
    parts = NORM_WIDTH // min(pieces[0].shape[0], 512)
    grid_spec = pltpu.PrefetchScalarGridSpec(
        num_scalar_prefetch=1,
        grid=(),
        in_specs=[vmem] * (len(pieces) + 4) + [whole] * len(earlier),
        out_specs=whole,
        scratch_shapes=[
            pltpu.VMEM((tokens, NORM_WIDTH), jnp.float32),
            pltpu.VMEM((tokens, NORM_WIDTH), jnp.bfloat16),
            pltpu.SemaphoreType.DMA((parts,)),
        ],
    )
    return pl.pallas_call(
        functools.partial(tail_kernel, base, len(earlier)),
        grid_spec=grid_spec,
        out_shape=jax.ShapeDtypeStruct(intra.shape, jnp.bfloat16),
        input_output_aliases={1 + len(pieces) + 4: 0} if earlier else {},
        compiler_params=pltpu.CompilerParams(vmem_limit_bytes=16 << 20),
        cost_estimate=pl.CostEstimate(flops=70_000_000, bytes_accessed=3_000_000, transcendentals=0),
    )(plan, *pieces, intra, carry, c_proj, gain, *earlier)


def plan_kernel(prefix_len, span_len, source_of, plan):
    me = lax.axis_index("dp")
    plan[CORE] = lax.axis_index("tensor")
    plan[ME] = me
    plan[PREFIX] = prefix_len[0]
    plan[SPAN] = span_len[0]
    for i in range(source_of.shape[0]):
        plan[TURNED + i] = source_of[i] ^ me


def plan_stage(prefix_len, span_len, source_of):
    smem = pl.BlockSpec(memory_space=pltpu.SMEM)
    return pl.pallas_call(
        plan_kernel,
        in_specs=[smem] * 3,
        out_specs=smem,
        out_shape=pltpu.SMEM((TURNED + source_of.shape[0],), jnp.int32),
        compiler_params=pltpu.CompilerParams(vmem_limit_bytes=1 << 20),
        name="plan_stage",
    )(prefix_len, span_len, source_of)


def cut_kernel(chosen, state, rims, *refs):
    pieces, rims_out, sems = refs[: len(chosen)], refs[-2], refs[-1]
    copies = []
    for i, (k, piece) in enumerate(zip(chosen, pieces)):
        copies.append(pltpu.make_async_copy(state.at[k], piece, sems.at[i]))
    copies.append(pltpu.make_async_copy(rims, rims_out, sems.at[len(chosen)]))
    for copy in copies:
        copy.start()
    for copy in copies:
        copy.wait()


def cut_stage(state, rims, chosen):
    return pl.pallas_call(
        functools.partial(cut_kernel, chosen),
        in_specs=[pl.BlockSpec(memory_space=pltpu.HBM)] * 2,
        out_specs=[pl.BlockSpec(memory_space=pltpu.VMEM)] * (len(chosen) + 1),
        out_shape=[pltpu.VMEM(state.shape[1:], state.dtype)] * len(chosen) + [pltpu.VMEM(rims.shape, rims.dtype)],
        scratch_shapes=[pltpu.SemaphoreType.DMA((len(chosen) + 1,))],
        compiler_params=pltpu.CompilerParams(vmem_limit_bytes=8 << 20),
        name="cut_stage",
    )(*keep_in(pltpu.HBM, state, rims))


def pick_kernel(order, column_count, plan, *refs):
    count = len(order)
    held, column = refs[:count], refs[count : count + column_count]
    slots, rim_out = refs[count + column_count : -1], refs[-1]
    for slot, k in zip(slots, order):
        wanted = plan[TURNED + (plan[ME] ^ k)]
        for r in range(count):

            @pl.when(wanted == r)
            def _(slot=slot, r=r):
                slot[...] = held[r][...]

    wanted = plan[TURNED + (plan[ME] ^ 1)] // 2
    for i in range(column_count):

        @pl.when(wanted == i)
        def _(i=i):
            rim_out[...] = column[i][...]


def pick_stage(plan, held, column, order):
    vmem = pl.BlockSpec(memory_space=pltpu.VMEM)
    grid_spec = pltpu.PrefetchScalarGridSpec(
        num_scalar_prefetch=1,
        grid=(),
        in_specs=[vmem] * (len(held) + len(column)),
        out_specs=[vmem] * (len(order) + 1),
    )
    shape = pltpu.VMEM(held[0].shape, held[0].dtype)
    return pl.pallas_call(
        functools.partial(pick_kernel, tuple(order), len(column)),
        grid_spec=grid_spec,
        out_shape=[shape] * len(order) + [pltpu.VMEM(column[0].shape, column[0].dtype)],
        compiler_params=pltpu.CompilerParams(vmem_limit_bytes=8 << 20),
        name="pick_stage",
    )(plan, *keep_in(pltpu.VMEM, *held), *keep_in(pltpu.VMEM, *column))


def column_rims(conv_store, own_rims):
    count = lax.axis_size("dp")
    held = {0: conv_store}
    step = count - 2
    bit = count // 2
    while bit > 1:
        for k in sorted(held):
            held[k ^ step] = swap(held[k], "dp", step)
        held[0] = own_rims
        bit //= 2
        step = bit
    return [held[2 * i] for i in range(count // 2)]


def gather_rims(conv_store, source_of, me):
    count = lax.axis_size("dp")
    held = conv_store
    index = jnp.zeros((), jnp.int32)
    away = source_of[me] ^ me
    bit = count // 2
    place = 1
    while bit > 0:
        held = jnp.concatenate([held, swap(held, "dp", bit)], axis=0)
        index = index + place * ((away // bit) & 1)
        bit //= 2
        place *= 2
    return lax.dynamic_index_in_dim(held, index, 0)


def local(
    xbc,
    gate_z,
    dt_raw,
    conv_weight,
    conv_bias,
    dt_bias,
    decay_rate,
    d_skip,
    norm_gain,
    ssm_store,
    conv_store,
    source_of,
    prefix_len,
    span_len,
):
    me = lax.axis_index("dp").astype(jnp.int32)
    owners = lax.axis_size("dp")
    direct = owners <= DIRECT_MAX
    order = offsets(owners)
    plan = plan_stage(prefix_len, span_len, source_of)
    state = ssm_store.reshape(owners, -1, STATE)
    if direct:
        held = [None] * owners
        opening = owners - 2
        every = [opening] + [k for k in order if k != opening] + [0]
        *pieces, own_rims = cut_stage(state, conv_store, every[1:])
        column = column_rims(conv_store, own_rims)
        for k, piece in zip(every, [state[every[0]]] + pieces):
            held[k] = swap(piece, "dp", k) if k else piece
        got = [None] * owners
        *picked, rim = pick_stage(plan, held, column, every)
        for k, piece in zip(every, picked):
            got[k] = swap(piece, "dp", k) if k else piece
        rims = column + [swap(rim, "dp", 1)]
    else:
        rims = [gather_rims(conv_store, source_of, me)]
        held = lax.all_to_all(state, "dp", split_axis=0, concat_axis=0, tiled=True)
        picked = jnp.take(held, source_of, axis=0)
        arrived = lax.all_to_all(picked, "dp", split_axis=0, concat_axis=0, tiled=True)
        got = list(arrived.reshape(-1, NORM_WIDTH, STATE))

    peer_xbc = swap(xbc, "tensor", 1)
    peer_gate = swap(gate_z, "tensor", 1)
    peer_dt = swap(dt_raw, "tensor", 1)
    intra, carry, c_proj = main_stage(
        plan,
        d_skip,
        xbc,
        peer_xbc,
        conv_weight,
        conv_bias.reshape(1, -1),
        gate_z,
        peer_gate,
        dt_raw,
        peer_dt,
        dt_bias,
        decay_rate,
        rims,
    )
    gain = norm_gain.reshape(1, -1)
    mixed = None
    norms = norm_gain.shape[0] // NORM_WIDTH
    share = len(got) // norms
    for base in range(norms):
        mine = got[base * share : (base + 1) * share]
        mixed = tail_stage(base, plan, mine, intra, carry, c_proj, gain, mixed)
    return mixed


def solution(mesh):
    in_specs = (
        P(("groups", "dp", "tensor"), None),
        P(("groups", "dp", "tensor"), None),
        P(("groups", "dp", "tensor"), None),
        P(),
        P(),
        P("tensor"),
        P("tensor"),
        P("tensor"),
        P("tensor"),
        P(("groups", "dp"), "tensor", None, None),
        P(("groups", "dp"), None, "tensor"),
        P("groups"),
        P(("groups", "dp")),
        P(("groups", "dp")),
    )
    out_specs = P(("groups", "dp"), "tensor")

    return jax.shard_map(local, mesh=mesh, in_specs=in_specs, out_specs=out_specs, check_vma=False)
```

```python
import functools

import jax
import jax.numpy as jnp
from jax import lax
from jax.experimental import pallas as pl
from jax.experimental.pallas import tpu as pltpu
from jax.sharding import PartitionSpec as P


HEAD_DIM = 64
STATE = 128
NORM_WIDTH = 2048
EPSILON = 1e-05
LANES = 128
DIRECT_MAX = 8


def swap(value, axis, offset):
    count = lax.axis_size(axis)
    return lax.ppermute(value, axis, [(i, i ^ offset) for i in range(count)])


CORE, ME, PREFIX, SPAN, TURNED = 0, 1, 2, 3, 4


def silu(value):
    half = 0.5 * value
    return half + half * jnp.tanh(half)


def keep_in(space, *values):
    return [pltpu.with_memory_space_constraint(value, space) for value in values]


def offsets(count):
    return sorted(range(1, count), key=lambda k: (-(k.bit_length()), k))


def main_kernel(
    rims_count,
    plan,
    skip_ref,
    own_x,
    peer_x,
    own_bc,
    peer_bc,
    weight_x,
    weight_bc,
    bias_x,
    bias_bc,
    own_gate,
    peer_gate,
    own_dt,
    peer_dt,
    dt_bias,
    decay_rate,
    *refs,
):
    rims = refs[:rims_count]
    intra_out, carry_out, c_out, extended, gates, scores, columns, cum_rows, step_rows = refs[rims_count:]
    block = pl.program_id(0)
    half, width = own_x.shape
    count = 2 * half
    per_block = width // HEAD_DIM
    groups = c_out.shape[1] // STATE
    blocks = pl.num_programs(0)
    live = plan[PREFIX] > 0
    taps = weight_x.shape[0]
    pad = 8 - (taps - 1)
    mine = pl.multiple_of(plan[CORE] * half, half)
    theirs = pl.multiple_of(half - mine, half)

    def edges(at):
        lanes = pl.ds(pl.multiple_of(at * width, width), width)
        edge = rims[0][0, :, lanes]
        if rims_count > 1:
            away = plan[TURNED + plan[ME]]
            choice = jnp.where((away & 1) == 0, away // 2, rims_count - 1)
            for i in range(1, rims_count):
                edge = jnp.where(choice == i, rims[i][0, :, lanes], edge)
        edge = edge.astype(jnp.float32)
        return jnp.where(live, edge, jnp.zeros_like(edge))

    def convolve(own, peer, at, weight, bias):
        extended[pad:8, :] = edges(at)
        extended[pl.ds(8 + mine, half), :] = own[...].astype(jnp.float32)
        extended[pl.ds(8 + theirs, half), :] = peer[...].astype(jnp.float32)
        total = jnp.broadcast_to(bias[...], (count, width))
        for k in range(taps):
            total = total + weight[k : k + 1, :] * extended[pad + k : pad + k + count, :]
        return silu(total).astype(jnp.bfloat16)

    row = lax.broadcasted_iota(jnp.int32, (count, LANES), 0)
    lane = lax.broadcasted_iota(jnp.int32, (count, LANES), 1)

    @pl.when(block == 0)
    def _():
        active = convolve(own_bc, peer_bc, blocks, weight_bc, bias_bc)
        c_out[...] = active[:, groups * STATE :]
        for g in range(groups):
            b = active[:, g * STATE : (g + 1) * STATE]
            c = active[:, (groups + g) * STATE : (groups + g + 1) * STATE]
            product = lax.dot_general(
                c, b, (((1,), (1,)), ((), ())), preferred_element_type=jnp.float32
            )
            scores[g] = jnp.where(row >= lane, product, 0.0)
        extended[pl.ds(8 + mine, half), :LANES] = own_dt[...].astype(jnp.float32)
        extended[pl.ds(8 + theirs, half), :LANES] = peer_dt[...].astype(jnp.float32)
        raw = extended[8 : 8 + count, :LANES]
        raw = jnp.where(plan[CORE] == 0, raw, pltpu.roll(raw, LANES // 2, 1))
        spare = jnp.zeros((1, LANES - dt_bias.shape[1]), jnp.float32)
        step = jax.nn.softplus(raw + jnp.concatenate([dt_bias[...], spare], axis=1))
        total = -jnp.concatenate([decay_rate[...], spare], axis=1) * step
        shift = 1
        while shift < count:
            total = total + jnp.where(row >= shift, pltpu.roll(total, shift, 0), 0.0)
            shift *= 2
        cum_rows[...] = total.T
        step_rows[...] = step.T
        for i in range(columns.shape[0]):
            columns[i] = total[:, i * per_block : (i + 1) * per_block]

    active = convolve(own_x, peer_x, block, weight_x, bias_x)
    gates[pl.ds(mine, half), :] = silu(own_gate[...].astype(jnp.float32))
    gates[pl.ds(theirs, half), :] = silu(peer_gate[...].astype(jnp.float32))
    score = scores[block // (blocks // groups)]
    column = columns[block]
    at = pl.multiple_of(block * per_block, per_block)
    cum_row = cum_rows[pl.ds(at, per_block), :]
    step_row = step_rows[pl.ds(at, per_block), :]
    left = lane < HEAD_DIM
    scale = jnp.where(live, 1.0, 0.0)
    for pair in range(per_block // 2):
        spread, weights = [], []
        for j in (2 * pair, 2 * pair + 1):
            cum = jnp.broadcast_to(column[:, j : j + 1], (count, LANES))
            decay = jnp.exp(jnp.minimum(cum - cum_row[j : j + 1, :], 0.0))
            weights.append((decay * score * step_row[j : j + 1, :]).astype(jnp.bfloat16))
            spread.append(cum)
        lanes = slice(pair * LANES, (pair + 1) * LANES)
        x = active[:, lanes]
        zero = jnp.zeros_like(x)
        stacked = jnp.concatenate([jnp.where(left, x, zero), jnp.where(left, zero, x)], axis=0)
        intra = lax.dot_general(
            jnp.concatenate(weights, axis=1),
            stacked,
            (((1,), (0,)), ((), ())),
            preferred_element_type=jnp.float32,
        )
        skip = jnp.where(left, skip_ref[at + 2 * pair], skip_ref[at + 2 * pair + 1])
        gate = gates[:, lanes]
        intra_out[:, lanes] = (intra + skip * x.astype(jnp.float32)) * gate
        decayed = jnp.exp(jnp.where(left, spread[0], spread[1]))
        carry_out[:, lanes] = gate * decayed * scale


def main_stage(plan, d_skip, xbc, peer_xbc, weight, bias, gate, peer_gate, dt, peer_dt, dt_bias, decay_rate, rims):
    rows, channels = xbc.shape
    half = channels // 2
    count = 2 * rows
    inner = gate.shape[1] // 2
    width = half - inner
    groups = width // (2 * STATE)
    blocks = inner // width
    per_half = half // width
    per_inner = inner // width
    heads = dt_bias.shape[0]
    at_x = lambda i, plan, *_: (0, plan[CORE] * per_half + i)
    at_bc = lambda i, plan, *_: (0, plan[CORE] * per_half + blocks)
    at_gate = lambda i, plan, *_: (0, plan[CORE] * per_inner + i)
    fixed = lambda i, *_: (0, 0)
    step = lambda i, *_: (0, i)
    taps = weight.shape[0]
    token = lambda index: pl.BlockSpec((rows, width), index)
    grid_spec = pltpu.PrefetchScalarGridSpec(
        num_scalar_prefetch=2,
        grid=(blocks,),
        in_specs=[
            token(at_x),
            token(at_x),
            token(at_bc),
            token(at_bc),
            pl.BlockSpec((taps, width), at_x),
            pl.BlockSpec((taps, width), at_bc),
            pl.BlockSpec((1, width), at_x),
            pl.BlockSpec((1, width), at_bc),
            token(at_gate),
            token(at_gate),
            pl.BlockSpec((rows, LANES), fixed),
            pl.BlockSpec((rows, LANES), fixed),
            pl.BlockSpec((1, heads), fixed),
            pl.BlockSpec((1, heads), fixed),
        ]
        + [pl.BlockSpec((1, taps - 1, half), lambda i, *_: (0, 0, 0))] * len(rims),
        out_specs=[
            pl.BlockSpec((count, width), step),
            pl.BlockSpec((count, width), step),
            pl.BlockSpec((count, groups * STATE), fixed),
        ],
        scratch_shapes=[
            pltpu.VMEM((count + 8, width), jnp.float32),
            pltpu.VMEM((count, width), jnp.float32),
            pltpu.VMEM((groups, count, LANES), jnp.float32),
            pltpu.VMEM((blocks, count, width // HEAD_DIM), jnp.float32),
            pltpu.VMEM((LANES, count), jnp.float32),
            pltpu.VMEM((LANES, count), jnp.float32),
        ],
    )
    xbc, gate = keep_in(pltpu.HBM, xbc, gate)
    return pl.pallas_call(
        functools.partial(main_kernel, len(rims)),
        grid_spec=grid_spec,
        out_shape=[
            jax.ShapeDtypeStruct((count, inner), jnp.float32),
            jax.ShapeDtypeStruct((count, inner), jnp.float32),
            jax.ShapeDtypeStruct((count, groups * STATE), jnp.bfloat16),
        ],
        compiler_params=pltpu.CompilerParams(vmem_limit_bytes=16 << 20),
        cost_estimate=pl.CostEstimate(flops=400_000_000, bytes_accessed=8_000_000, transcendentals=2_000_000),
        name="main_stage",
    )(
        plan,
        d_skip,
        xbc,
        peer_xbc,
        xbc,
        peer_xbc,
        weight,
        weight,
        bias,
        bias,
        gate,
        peer_gate,
        dt,
        peer_dt,
        dt_bias.reshape(1, -1),
        decay_rate.reshape(1, -1),
        *rims,
    )


def tail_kernel(base, piece_count, last, plan, *refs):
    pieces, refs = refs[:piece_count], refs[piece_count:]
    intra, carry, c_proj, gain = refs[:4]
    before, refs = (refs[4 : 4 + base], refs[4 + base :]) if last else ((), refs[4:])
    out, wide = refs[:2]
    tokens = wide.shape[0]
    count, rows = len(pieces), pieces[0].shape[0]
    turn = plan[TURNED + plan[ME]] if count > 1 else 0
    group = base ^ (turn // count)
    within = turn % count
    keep = lax.broadcasted_iota(jnp.int32, (tokens, 1), 0) < plan[SPAN]
    narrow, sems = (refs[2], refs[3]) if last else (out, None)
    copies = []
    for earlier, part_out in enumerate(before):
        column = pl.multiple_of((earlier ^ (turn // count)) * NORM_WIDTH, NORM_WIDTH)
        copies.append(pltpu.make_async_copy(part_out, out.at[:, pl.ds(column, NORM_WIDTH)], sems.at[earlier]))
        copies[-1].start()
    c = c_proj[:, pl.ds(pl.multiple_of(group * STATE, STATE), STATE)]
    part = min(rows, 512)
    total = jnp.zeros((tokens, 1), jnp.float32)
    places = []
    for k, piece in enumerate(pieces):
        for at in range(0, rows, part):
            local_at = pl.multiple_of((k ^ within) * rows + at, part)
            column = pl.multiple_of(group * NORM_WIDTH + local_at, part)
            carried = lax.dot_general(
                c, piece[at : at + part, :], (((1,), (1,)), ((), ())), preferred_element_type=jnp.float32
            )
            value = intra[:, pl.ds(column, part)] + carry[:, pl.ds(column, part)] * carried
            total = total + jnp.sum(value * value, axis=1, keepdims=True)
            index = len(places)
            wide[:, index * part : (index + 1) * part] = value
            places.append(column)
    scale = lax.rsqrt(total * (1.0 / NORM_WIDTH) + EPSILON)
    for index, column in enumerate(places):
        lanes = slice(index * part, (index + 1) * part)
        normed = wide[:, lanes] * scale * gain[:, pl.ds(column, part)]
        value = jnp.where(keep, normed, 0.0).astype(jnp.bfloat16)
        if last:
            narrow[:, lanes] = value
            target = out.at[:, pl.ds(column, part)]
            copies.append(pltpu.make_async_copy(narrow.at[:, lanes], target, sems.at[base + index]))
            copies[-1].start()
        else:
            narrow[:, pl.ds(pl.multiple_of(column - group * NORM_WIDTH, part), part)] = value
    for copy in copies:
        copy.wait()


def tail_stage(base, last, plan, pieces, intra, carry, c_proj, gain, before):
    tokens, _ = intra.shape
    vmem = pl.BlockSpec(memory_space=pltpu.VMEM)
    parts = NORM_WIDTH // min(pieces[0].shape[0], 512)
    earlier = before if last else []
    scratch = [pltpu.VMEM((tokens, NORM_WIDTH), jnp.float32)]
    if last:
        scratch += [pltpu.VMEM((tokens, NORM_WIDTH), jnp.bfloat16), pltpu.SemaphoreType.DMA((base + parts,))]
        out_shape = jax.ShapeDtypeStruct(intra.shape, jnp.bfloat16)
    else:
        out_shape = pltpu.VMEM((tokens, NORM_WIDTH), jnp.bfloat16)
    grid_spec = pltpu.PrefetchScalarGridSpec(
        num_scalar_prefetch=1,
        grid=(),
        in_specs=[vmem] * (len(pieces) + 4 + len(earlier)),
        out_specs=pl.BlockSpec(memory_space=pltpu.HBM) if last else vmem,
        scratch_shapes=scratch,
    )
    return pl.pallas_call(
        functools.partial(tail_kernel, base, len(pieces), last),
        grid_spec=grid_spec,
        out_shape=out_shape,
        compiler_params=pltpu.CompilerParams(vmem_limit_bytes=16 << 20),
        cost_estimate=pl.CostEstimate(flops=70_000_000, bytes_accessed=3_000_000, transcendentals=0),
    )(plan, *pieces, intra, carry, c_proj, gain, *earlier)


def plan_kernel(prefix_len, span_len, source_of, plan):
    me = lax.axis_index("dp")
    plan[CORE] = lax.axis_index("tensor")
    plan[ME] = me
    plan[PREFIX] = prefix_len[0]
    plan[SPAN] = span_len[0]
    for i in range(source_of.shape[0]):
        plan[TURNED + i] = source_of[i] ^ me


def plan_stage(prefix_len, span_len, source_of):
    smem = pl.BlockSpec(memory_space=pltpu.SMEM)
    return pl.pallas_call(
        plan_kernel,
        in_specs=[smem] * 3,
        out_specs=smem,
        out_shape=pltpu.SMEM((TURNED + source_of.shape[0],), jnp.int32),
        compiler_params=pltpu.CompilerParams(vmem_limit_bytes=1 << 20),
        name="plan_stage",
    )(prefix_len, span_len, source_of)


def cut_kernel(chosen, state, rims, *refs):
    pieces, rims_out, sems = refs[: len(chosen)], refs[-2], refs[-1]
    copies = []
    for i, (k, piece) in enumerate(zip(chosen, pieces)):
        copies.append(pltpu.make_async_copy(state.at[k], piece, sems.at[i]))
    copies.append(pltpu.make_async_copy(rims, rims_out, sems.at[len(chosen)]))
    for copy in copies:
        copy.start()
    for copy in copies:
        copy.wait()


def cut_stage(state, rims, chosen):
    return pl.pallas_call(
        functools.partial(cut_kernel, chosen),
        in_specs=[pl.BlockSpec(memory_space=pltpu.HBM)] * 2,
        out_specs=[pl.BlockSpec(memory_space=pltpu.VMEM)] * (len(chosen) + 1),
        out_shape=[pltpu.VMEM(state.shape[1:], state.dtype)] * len(chosen) + [pltpu.VMEM(rims.shape, rims.dtype)],
        scratch_shapes=[pltpu.SemaphoreType.DMA((len(chosen) + 1,))],
        compiler_params=pltpu.CompilerParams(vmem_limit_bytes=8 << 20),
        name="cut_stage",
    )(*keep_in(pltpu.HBM, state, rims))


def pick_kernel(order, column_count, plan, *refs):
    count = len(order)
    held, column = refs[:count], refs[count : count + column_count]
    slots, rim_out = refs[count + column_count : -1], refs[-1]
    for slot, k in zip(slots, order):
        wanted = plan[TURNED + (plan[ME] ^ k)]
        for r in range(count):

            @pl.when(wanted == r)
            def _(slot=slot, r=r):
                slot[...] = held[r][...]

    wanted = plan[TURNED + (plan[ME] ^ 1)] // 2
    for i in range(column_count):

        @pl.when(wanted == i)
        def _(i=i):
            rim_out[...] = column[i][...]


def pick_stage(plan, held, column, order):
    vmem = pl.BlockSpec(memory_space=pltpu.VMEM)
    grid_spec = pltpu.PrefetchScalarGridSpec(
        num_scalar_prefetch=1,
        grid=(),
        in_specs=[vmem] * (len(held) + len(column)),
        out_specs=[vmem] * (len(order) + 1),
    )
    shape = pltpu.VMEM(held[0].shape, held[0].dtype)
    return pl.pallas_call(
        functools.partial(pick_kernel, tuple(order), len(column)),
        grid_spec=grid_spec,
        out_shape=[shape] * len(order) + [pltpu.VMEM(column[0].shape, column[0].dtype)],
        compiler_params=pltpu.CompilerParams(vmem_limit_bytes=8 << 20),
        name="pick_stage",
    )(plan, *keep_in(pltpu.VMEM, *held), *keep_in(pltpu.VMEM, *column))


def column_rims(conv_store, own_rims):
    count = lax.axis_size("dp")
    held = {0: conv_store}
    step = count - 2
    bit = count // 2
    while bit > 1:
        for k in sorted(held):
            held[k ^ step] = swap(held[k], "dp", step)
        held[0] = own_rims
        bit //= 2
        step = bit
    return [held[2 * i] for i in range(count // 2)]


def gather_rims(conv_store, source_of, me):
    count = lax.axis_size("dp")
    held = conv_store
    index = jnp.zeros((), jnp.int32)
    away = source_of[me] ^ me
    bit = count // 2
    place = 1
    while bit > 0:
        held = jnp.concatenate([held, swap(held, "dp", bit)], axis=0)
        index = index + place * ((away // bit) & 1)
        bit //= 2
        place *= 2
    return lax.dynamic_index_in_dim(held, index, 0)


def local(
    xbc,
    gate_z,
    dt_raw,
    conv_weight,
    conv_bias,
    dt_bias,
    decay_rate,
    d_skip,
    norm_gain,
    ssm_store,
    conv_store,
    source_of,
    prefix_len,
    span_len,
):
    me = lax.axis_index("dp").astype(jnp.int32)
    owners = lax.axis_size("dp")
    direct = owners <= DIRECT_MAX
    order = offsets(owners)
    plan = plan_stage(prefix_len, span_len, source_of)
    state = ssm_store.reshape(owners, -1, STATE)
    if direct:
        held = [None] * owners
        opening = owners - 2
        every = [opening] + [k for k in order if k != opening] + [0]
        *pieces, own_rims = cut_stage(state, conv_store, every[1:])
        column = column_rims(conv_store, own_rims)
        for k, piece in zip(every, [state[every[0]]] + pieces):
            held[k] = swap(piece, "dp", k) if k else piece
        got = [None] * owners
        *picked, rim = pick_stage(plan, held, column, every)
        for k, piece in zip(every, picked):
            got[k] = swap(piece, "dp", k) if k else piece
        rims = column + [swap(rim, "dp", 1)]
    else:
        rims = [gather_rims(conv_store, source_of, me)]
        held = lax.all_to_all(state, "dp", split_axis=0, concat_axis=0, tiled=True)
        picked = jnp.take(held, source_of, axis=0)
        arrived = lax.all_to_all(picked, "dp", split_axis=0, concat_axis=0, tiled=True)
        got = list(arrived.reshape(-1, NORM_WIDTH, STATE))

    peer_xbc = swap(xbc, "tensor", 1)
    peer_gate = swap(gate_z, "tensor", 1)
    peer_dt = swap(dt_raw, "tensor", 1)
    intra, carry, c_proj = main_stage(
        plan,
        d_skip,
        xbc,
        peer_xbc,
        conv_weight,
        conv_bias.reshape(1, -1),
        gate_z,
        peer_gate,
        dt_raw,
        peer_dt,
        dt_bias,
        decay_rate,
        rims,
    )
    gain = norm_gain.reshape(1, -1)
    norms = norm_gain.shape[0] // NORM_WIDTH
    share = len(got) // norms
    done = []
    for base in range(norms):
        mine = got[base * share : (base + 1) * share]
        done.append(tail_stage(base, base == norms - 1, plan, mine, intra, carry, c_proj, gain, done))
    return done[-1]


def solution(mesh):
    in_specs = (
        P(("groups", "dp", "tensor"), None),
        P(("groups", "dp", "tensor"), None),
        P(("groups", "dp", "tensor"), None),
        P(),
        P(),
        P("tensor"),
        P("tensor"),
        P("tensor"),
        P("tensor"),
        P(("groups", "dp"), "tensor", None, None),
        P(("groups", "dp"), None, "tensor"),
        P("groups"),
        P(("groups", "dp")),
        P(("groups", "dp")),
    )
    out_specs = P(("groups", "dp"), "tensor")

    return jax.shard_map(local, mesh=mesh, in_specs=in_specs, out_specs=out_specs, check_vma=False)
```

```python
import functools

import jax
import jax.numpy as jnp
from jax import lax
from jax.experimental import pallas as pl
from jax.experimental.pallas import tpu as pltpu
from jax.sharding import PartitionSpec as P


HEAD_DIM = 64
STATE = 128
NORM_WIDTH = 2048
EPSILON = 1e-05
LANES = 128
DIRECT_MAX = 8


def swap(value, axis, offset):
    count = lax.axis_size(axis)
    return lax.ppermute(value, axis, [(i, i ^ offset) for i in range(count)])


CORE, ME, PREFIX, SPAN, TURNED = 0, 1, 2, 3, 4


def silu(value):
    half = 0.5 * value
    return half + half * jnp.tanh(half)


def keep_in(space, *values):
    return [pltpu.with_memory_space_constraint(value, space) for value in values]


def offsets(count):
    return sorted(range(1, count), key=lambda k: (-(k.bit_length()), k))


def main_kernel(
    rims_count,
    plan,
    skip_ref,
    own_x,
    peer_x,
    own_bc,
    peer_bc,
    weight_x,
    weight_bc,
    bias_x,
    bias_bc,
    own_gate,
    peer_gate,
    own_dt,
    peer_dt,
    dt_bias,
    decay_rate,
    *refs,
):
    rims = refs[:rims_count]
    intra_out, carry_out, c_out, extended, gates, scores, columns, cum_rows, step_rows = refs[rims_count:]
    block = pl.program_id(0)
    half, width = own_x.shape
    count = 2 * half
    per_block = width // HEAD_DIM
    groups = c_out.shape[1] // STATE
    blocks = pl.num_programs(0)
    live = plan[PREFIX] > 0
    taps = weight_x.shape[0]
    pad = 8 - (taps - 1)
    mine = pl.multiple_of(plan[CORE] * half, half)
    theirs = pl.multiple_of(half - mine, half)

    def edges(at):
        lanes = pl.ds(pl.multiple_of(at * width, width), width)
        edge = rims[0][0, :, lanes]
        if rims_count > 1:
            away = plan[TURNED + plan[ME]]
            choice = jnp.where((away & 1) == 0, away // 2, rims_count - 1)
            for i in range(1, rims_count):
                edge = jnp.where(choice == i, rims[i][0, :, lanes], edge)
        edge = edge.astype(jnp.float32)
        return jnp.where(live, edge, jnp.zeros_like(edge))

    def convolve(own, peer, at, weight, bias):
        extended[pad:8, :] = edges(at)
        extended[pl.ds(8 + mine, half), :] = own[...].astype(jnp.float32)
        extended[pl.ds(8 + theirs, half), :] = peer[...].astype(jnp.float32)
        total = jnp.broadcast_to(bias[...], (count, width))
        for k in range(taps):
            total = total + weight[k : k + 1, :] * extended[pad + k : pad + k + count, :]
        return silu(total).astype(jnp.bfloat16)

    row = lax.broadcasted_iota(jnp.int32, (count, LANES), 0)
    lane = lax.broadcasted_iota(jnp.int32, (count, LANES), 1)

    @pl.when(block == 0)
    def _():
        active = convolve(own_bc, peer_bc, blocks, weight_bc, bias_bc)
        c_out[...] = active[:, groups * STATE :]
        for g in range(groups):
            b = active[:, g * STATE : (g + 1) * STATE]
            c = active[:, (groups + g) * STATE : (groups + g + 1) * STATE]
            product = lax.dot_general(
                c, b, (((1,), (1,)), ((), ())), preferred_element_type=jnp.float32
            )
            scores[g] = jnp.where(row >= lane, product, 0.0)
        extended[pl.ds(8 + mine, half), :LANES] = own_dt[...].astype(jnp.float32)
        extended[pl.ds(8 + theirs, half), :LANES] = peer_dt[...].astype(jnp.float32)
        raw = extended[8 : 8 + count, :LANES]
        raw = jnp.where(plan[CORE] == 0, raw, pltpu.roll(raw, LANES // 2, 1))
        spare = jnp.zeros((1, LANES - dt_bias.shape[1]), jnp.float32)
        step = jax.nn.softplus(raw + jnp.concatenate([dt_bias[...], spare], axis=1))
        total = -jnp.concatenate([decay_rate[...], spare], axis=1) * step
        shift = 1
        while shift < count:
            total = total + jnp.where(row >= shift, pltpu.roll(total, shift, 0), 0.0)
            shift *= 2
        cum_rows[...] = total.T
        step_rows[...] = step.T
        for i in range(columns.shape[0]):
            columns[i] = total[:, i * per_block : (i + 1) * per_block]

    active = convolve(own_x, peer_x, block, weight_x, bias_x)
    gates[pl.ds(mine, half), :] = silu(own_gate[...].astype(jnp.float32))
    gates[pl.ds(theirs, half), :] = silu(peer_gate[...].astype(jnp.float32))
    score = scores[block // (blocks // groups)]
    column = columns[block]
    at = pl.multiple_of(block * per_block, per_block)
    cum_row = cum_rows[pl.ds(at, per_block), :]
    step_row = step_rows[pl.ds(at, per_block), :]
    left = lane < HEAD_DIM
    scale = jnp.where(live, 1.0, 0.0)
    for pair in range(per_block // 2):
        spread, weights = [], []
        for j in (2 * pair, 2 * pair + 1):
            cum = jnp.broadcast_to(column[:, j : j + 1], (count, LANES))
            decay = jnp.exp(jnp.minimum(cum - cum_row[j : j + 1, :], 0.0))
            weights.append((decay * score * step_row[j : j + 1, :]).astype(jnp.bfloat16))
            spread.append(cum)
        lanes = slice(pair * LANES, (pair + 1) * LANES)
        x = active[:, lanes]
        zero = jnp.zeros_like(x)
        stacked = jnp.concatenate([jnp.where(left, x, zero), jnp.where(left, zero, x)], axis=0)
        intra = lax.dot_general(
            jnp.concatenate(weights, axis=1),
            stacked,
            (((1,), (0,)), ((), ())),
            preferred_element_type=jnp.float32,
        )
        skip = jnp.where(left, skip_ref[at + 2 * pair], skip_ref[at + 2 * pair + 1])
        gate = gates[:, lanes]
        intra_out[:, lanes] = (intra + skip * x.astype(jnp.float32)) * gate
        decayed = jnp.exp(jnp.where(left, spread[0], spread[1]))
        carry_out[:, lanes] = gate * decayed * scale


def main_stage(plan, d_skip, xbc, peer_xbc, weight, bias, gate, peer_gate, dt, peer_dt, dt_bias, decay_rate, rims):
    rows, channels = xbc.shape
    half = channels // 2
    count = 2 * rows
    inner = gate.shape[1] // 2
    width = half - inner
    groups = width // (2 * STATE)
    blocks = inner // width
    per_half = half // width
    per_inner = inner // width
    heads = dt_bias.shape[0]
    at_x = lambda i, plan, *_: (0, plan[CORE] * per_half + i)
    at_bc = lambda i, plan, *_: (0, plan[CORE] * per_half + blocks)
    at_gate = lambda i, plan, *_: (0, plan[CORE] * per_inner + i)
    fixed = lambda i, *_: (0, 0)
    step = lambda i, *_: (0, i)
    taps = weight.shape[0]
    token = lambda index: pl.BlockSpec((rows, width), index)
    grid_spec = pltpu.PrefetchScalarGridSpec(
        num_scalar_prefetch=2,
        grid=(blocks,),
        in_specs=[
            token(at_x),
            token(at_x),
            token(at_bc),
            token(at_bc),
            pl.BlockSpec((taps, width), at_x),
            pl.BlockSpec((taps, width), at_bc),
            pl.BlockSpec((1, width), at_x),
            pl.BlockSpec((1, width), at_bc),
            token(at_gate),
            token(at_gate),
            pl.BlockSpec((rows, LANES), fixed),
            pl.BlockSpec((rows, LANES), fixed),
            pl.BlockSpec((1, heads), fixed),
            pl.BlockSpec((1, heads), fixed),
        ]
        + [pl.BlockSpec((1, taps - 1, half), lambda i, *_: (0, 0, 0))] * len(rims),
        out_specs=[
            pl.BlockSpec((count, width), step),
            pl.BlockSpec((count, width), step),
            pl.BlockSpec((count, groups * STATE), fixed),
        ],
        scratch_shapes=[
            pltpu.VMEM((count + 8, width), jnp.float32),
            pltpu.VMEM((count, width), jnp.float32),
            pltpu.VMEM((groups, count, LANES), jnp.float32),
            pltpu.VMEM((blocks, count, width // HEAD_DIM), jnp.float32),
            pltpu.VMEM((LANES, count), jnp.float32),
            pltpu.VMEM((LANES, count), jnp.float32),
        ],
    )
    xbc, gate = keep_in(pltpu.HBM, xbc, gate)
    return pl.pallas_call(
        functools.partial(main_kernel, len(rims)),
        grid_spec=grid_spec,
        out_shape=[
            jax.ShapeDtypeStruct((count, inner), jnp.float32),
            jax.ShapeDtypeStruct((count, inner), jnp.float32),
            jax.ShapeDtypeStruct((count, groups * STATE), jnp.bfloat16),
        ],
        compiler_params=pltpu.CompilerParams(vmem_limit_bytes=16 << 20),
        cost_estimate=pl.CostEstimate(flops=400_000_000, bytes_accessed=8_000_000, transcendentals=2_000_000),
        name="main_stage",
    )(
        plan,
        d_skip,
        xbc,
        peer_xbc,
        xbc,
        peer_xbc,
        weight,
        weight,
        bias,
        bias,
        gate,
        peer_gate,
        dt,
        peer_dt,
        dt_bias.reshape(1, -1),
        decay_rate.reshape(1, -1),
        *rims,
    )


def early_kernel(base, count, plan, *refs):
    intra, carry, c_proj, values, squares = refs[-5:]
    pieces = refs[:-5]
    rows = pieces[0].shape[0]
    turn = plan[TURNED + plan[ME]]
    group = base ^ (turn // count)
    c = c_proj[:, pl.ds(pl.multiple_of(group * STATE, STATE), STATE)]
    total = jnp.zeros((c.shape[0], 1), jnp.float32)
    for k, piece in enumerate(pieces):
        column = pl.multiple_of(group * NORM_WIDTH + (k ^ (turn % count)) * rows, rows)
        carried = lax.dot_general(
            c, piece[...], (((1,), (1,)), ((), ())), preferred_element_type=jnp.float32
        )
        value = intra[:, pl.ds(column, rows)] + carry[:, pl.ds(column, rows)] * carried
        total = total + jnp.sum(value * value, axis=1, keepdims=True)
        values[:, k * rows : (k + 1) * rows] = value
    squares[...] = jnp.broadcast_to(total, squares.shape)


def early_stage(base, count, plan, pieces, intra, carry, c_proj):
    tokens = intra.shape[0]
    vmem = pl.BlockSpec(memory_space=pltpu.VMEM)
    return pl.pallas_call(
        functools.partial(early_kernel, base, count),
        grid_spec=pltpu.PrefetchScalarGridSpec(
            num_scalar_prefetch=1, grid=(), in_specs=[vmem] * (len(pieces) + 3), out_specs=[vmem] * 2
        ),
        out_shape=[
            pltpu.VMEM((tokens, len(pieces) * pieces[0].shape[0]), jnp.float32),
            pltpu.VMEM((tokens, LANES), jnp.float32),
        ],
        compiler_params=pltpu.CompilerParams(vmem_limit_bytes=16 << 20),
        name="early_stage",
    )(plan, *pieces, intra, carry, c_proj)


def tail_kernel(base, piece_count, last, plan, *refs):
    pieces, refs = refs[:piece_count], refs[piece_count:]
    intra, carry, c_proj, gain = refs[:4]
    before, refs = (refs[4 : 4 + base], refs[4 + base :]) if last else ((), refs[4:])
    out, wide = refs[:2]
    tokens = wide.shape[0]
    rows = pieces[-1].shape[0]
    count = NORM_WIDTH // rows
    turn = plan[TURNED + plan[ME]] if count > 1 else 0
    group = base ^ (turn // count)
    within = turn % count
    keep = lax.broadcasted_iota(jnp.int32, (tokens, 1), 0) < plan[SPAN]
    narrow, sems = (refs[2], refs[3]) if last else (out, None)
    copies = []
    for earlier, part_out in enumerate(before):
        column = pl.multiple_of((earlier ^ (turn // count)) * NORM_WIDTH, NORM_WIDTH)
        copies.append(pltpu.make_async_copy(part_out, out.at[:, pl.ds(column, NORM_WIDTH)], sems.at[earlier]))
        copies[-1].start()
    c = c_proj[:, pl.ds(pl.multiple_of(group * STATE, STATE), STATE)]
    part = min(rows, 512)
    total = jnp.zeros((tokens, 1), jnp.float32)
    places = []
    known = last and count > 1
    if known:
        total = total + pieces[1][:, :1]
    for k in range(count):
        for at in range(0, rows, part):
            local_at = pl.multiple_of((k ^ within) * rows + at, part)
            column = pl.multiple_of(group * NORM_WIDTH + local_at, part)
            if known and k < count - 1:
                places.append(column)
                continue
            piece = pieces[2] if known else pieces[k]
            carried = lax.dot_general(
                c, piece[at : at + part, :], (((1,), (1,)), ((), ())), preferred_element_type=jnp.float32
            )
            value = intra[:, pl.ds(column, part)] + carry[:, pl.ds(column, part)] * carried
            total = total + jnp.sum(value * value, axis=1, keepdims=True)
            index = len(places)
            wide[:, index * part : (index + 1) * part] = value
            places.append(column)
    scale = lax.rsqrt(total * (1.0 / NORM_WIDTH) + EPSILON)
    for index, column in enumerate(places):
        lanes = slice(index * part, (index + 1) * part)
        gated = pieces[0] if known and index < len(places) - 1 else wide
        normed = gated[:, lanes] * scale * gain[:, pl.ds(column, part)]
        value = jnp.where(keep, normed, 0.0).astype(jnp.bfloat16)
        if last:
            narrow[:, lanes] = value
            target = out.at[:, pl.ds(column, part)]
            copies.append(pltpu.make_async_copy(narrow.at[:, lanes], target, sems.at[base + index]))
            copies[-1].start()
        else:
            narrow[:, pl.ds(pl.multiple_of(column - group * NORM_WIDTH, part), part)] = value
    for copy in copies:
        copy.wait()


def tail_stage(base, last, plan, pieces, intra, carry, c_proj, gain, before):
    tokens, _ = intra.shape
    vmem = pl.BlockSpec(memory_space=pltpu.VMEM)
    parts = NORM_WIDTH // min(pieces[-1].shape[0], 512)
    earlier = before if last else []
    scratch = [pltpu.VMEM((tokens, NORM_WIDTH), jnp.float32)]
    if last:
        scratch += [pltpu.VMEM((tokens, NORM_WIDTH), jnp.bfloat16), pltpu.SemaphoreType.DMA((base + parts,))]
        out_shape = jax.ShapeDtypeStruct(intra.shape, jnp.bfloat16)
    else:
        out_shape = pltpu.VMEM((tokens, NORM_WIDTH), jnp.bfloat16)
    grid_spec = pltpu.PrefetchScalarGridSpec(
        num_scalar_prefetch=1,
        grid=(),
        in_specs=[vmem] * (len(pieces) + 4 + len(earlier)),
        out_specs=pl.BlockSpec(memory_space=pltpu.HBM) if last else vmem,
        scratch_shapes=scratch,
    )
    return pl.pallas_call(
        functools.partial(tail_kernel, base, len(pieces), last),
        grid_spec=grid_spec,
        out_shape=out_shape,
        compiler_params=pltpu.CompilerParams(vmem_limit_bytes=16 << 20),
        cost_estimate=pl.CostEstimate(flops=70_000_000, bytes_accessed=3_000_000, transcendentals=0),
    )(plan, *pieces, intra, carry, c_proj, gain, *earlier)


def plan_kernel(prefix_len, span_len, source_of, plan):
    me = lax.axis_index("dp")
    plan[CORE] = lax.axis_index("tensor")
    plan[ME] = me
    plan[PREFIX] = prefix_len[0]
    plan[SPAN] = span_len[0]
    for i in range(source_of.shape[0]):
        plan[TURNED + i] = source_of[i] ^ me


def plan_stage(prefix_len, span_len, source_of):
    smem = pl.BlockSpec(memory_space=pltpu.SMEM)
    return pl.pallas_call(
        plan_kernel,
        in_specs=[smem] * 3,
        out_specs=smem,
        out_shape=pltpu.SMEM((TURNED + source_of.shape[0],), jnp.int32),
        compiler_params=pltpu.CompilerParams(vmem_limit_bytes=1 << 20),
        name="plan_stage",
    )(prefix_len, span_len, source_of)


def cut_kernel(chosen, state, rims, *refs):
    pieces, rims_out, sems = refs[: len(chosen)], refs[-2], refs[-1]
    copies = []
    for i, (k, piece) in enumerate(zip(chosen, pieces)):
        copies.append(pltpu.make_async_copy(state.at[k], piece, sems.at[i]))
    copies.append(pltpu.make_async_copy(rims, rims_out, sems.at[len(chosen)]))
    for copy in copies:
        copy.start()
    for copy in copies:
        copy.wait()


def cut_stage(state, rims, chosen):
    return pl.pallas_call(
        functools.partial(cut_kernel, chosen),
        in_specs=[pl.BlockSpec(memory_space=pltpu.HBM)] * 2,
        out_specs=[pl.BlockSpec(memory_space=pltpu.VMEM)] * (len(chosen) + 1),
        out_shape=[pltpu.VMEM(state.shape[1:], state.dtype)] * len(chosen) + [pltpu.VMEM(rims.shape, rims.dtype)],
        scratch_shapes=[pltpu.SemaphoreType.DMA((len(chosen) + 1,))],
        compiler_params=pltpu.CompilerParams(vmem_limit_bytes=8 << 20),
        name="cut_stage",
    )(*keep_in(pltpu.HBM, state, rims))


def pick_kernel(order, column_count, plan, *refs):
    count = len(order)
    held, column = refs[:count], refs[count : count + column_count]
    slots, rim_out = refs[count + column_count : -1], refs[-1]
    for slot, k in zip(slots, order):
        wanted = plan[TURNED + (plan[ME] ^ k)]
        for r in range(count):

            @pl.when(wanted == r)
            def _(slot=slot, r=r):
                slot[...] = held[r][...]

    wanted = plan[TURNED + (plan[ME] ^ 1)] // 2
    for i in range(column_count):

        @pl.when(wanted == i)
        def _(i=i):
            rim_out[...] = column[i][...]


def pick_stage(plan, held, column, order):
    vmem = pl.BlockSpec(memory_space=pltpu.VMEM)
    grid_spec = pltpu.PrefetchScalarGridSpec(
        num_scalar_prefetch=1,
        grid=(),
        in_specs=[vmem] * (len(held) + len(column)),
        out_specs=[vmem] * (len(order) + 1),
    )
    shape = pltpu.VMEM(held[0].shape, held[0].dtype)
    return pl.pallas_call(
        functools.partial(pick_kernel, tuple(order), len(column)),
        grid_spec=grid_spec,
        out_shape=[shape] * len(order) + [pltpu.VMEM(column[0].shape, column[0].dtype)],
        compiler_params=pltpu.CompilerParams(vmem_limit_bytes=8 << 20),
        name="pick_stage",
    )(plan, *keep_in(pltpu.VMEM, *held), *keep_in(pltpu.VMEM, *column))


def column_rims(conv_store, own_rims):
    count = lax.axis_size("dp")
    held = {0: conv_store}
    step = count - 2
    bit = count // 2
    while bit > 1:
        for k in sorted(held):
            held[k ^ step] = swap(held[k], "dp", step)
        held[0] = own_rims
        bit //= 2
        step = bit
    return [held[2 * i] for i in range(count // 2)]


def gather_rims(conv_store, source_of, me):
    count = lax.axis_size("dp")
    held = conv_store
    index = jnp.zeros((), jnp.int32)
    away = source_of[me] ^ me
    bit = count // 2
    place = 1
    while bit > 0:
        held = jnp.concatenate([held, swap(held, "dp", bit)], axis=0)
        index = index + place * ((away // bit) & 1)
        bit //= 2
        place *= 2
    return lax.dynamic_index_in_dim(held, index, 0)


def local(
    xbc,
    gate_z,
    dt_raw,
    conv_weight,
    conv_bias,
    dt_bias,
    decay_rate,
    d_skip,
    norm_gain,
    ssm_store,
    conv_store,
    source_of,
    prefix_len,
    span_len,
):
    me = lax.axis_index("dp").astype(jnp.int32)
    owners = lax.axis_size("dp")
    direct = owners <= DIRECT_MAX
    order = offsets(owners)
    plan = plan_stage(prefix_len, span_len, source_of)
    state = ssm_store.reshape(owners, -1, STATE)
    if direct:
        held = [None] * owners
        opening = owners - 2
        every = [opening] + [k for k in order if k != opening] + [0]
        *pieces, own_rims = cut_stage(state, conv_store, every[1:])
        column = column_rims(conv_store, own_rims)
        for k, piece in zip(every, [state[every[0]]] + pieces):
            held[k] = swap(piece, "dp", k) if k else piece
        got = [None] * owners
        *picked, rim = pick_stage(plan, held, column, every)
        for k, piece in zip(every, picked):
            got[k] = swap(piece, "dp", k) if k else piece
        rims = column + [swap(rim, "dp", 1)]
    else:
        rims = [gather_rims(conv_store, source_of, me)]
        held = lax.all_to_all(state, "dp", split_axis=0, concat_axis=0, tiled=True)
        picked = jnp.take(held, source_of, axis=0)
        arrived = lax.all_to_all(picked, "dp", split_axis=0, concat_axis=0, tiled=True)
        got = list(arrived.reshape(-1, NORM_WIDTH, STATE))

    peer_xbc = swap(xbc, "tensor", 1)
    peer_gate = swap(gate_z, "tensor", 1)
    peer_dt = swap(dt_raw, "tensor", 1)
    intra, carry, c_proj = main_stage(
        plan,
        d_skip,
        xbc,
        peer_xbc,
        conv_weight,
        conv_bias.reshape(1, -1),
        gate_z,
        peer_gate,
        dt_raw,
        peer_dt,
        dt_bias,
        decay_rate,
        rims,
    )
    gain = norm_gain.reshape(1, -1)
    norms = norm_gain.shape[0] // NORM_WIDTH
    share = len(got) // norms
    done = []
    for base in range(norms):
        mine = got[base * share : (base + 1) * share]
        if direct and base == norms - 1:
            mine = [*early_stage(base, share, plan, mine[:-1], intra, carry, c_proj), mine[-1]]
        done.append(tail_stage(base, base == norms - 1, plan, mine, intra, carry, c_proj, gain, done))
    return done[-1]


def solution(mesh):
    in_specs = (
        P(("groups", "dp", "tensor"), None),
        P(("groups", "dp", "tensor"), None),
        P(("groups", "dp", "tensor"), None),
        P(),
        P(),
        P("tensor"),
        P("tensor"),
        P("tensor"),
        P("tensor"),
        P(("groups", "dp"), "tensor", None, None),
        P(("groups", "dp"), None, "tensor"),
        P("groups"),
        P(("groups", "dp")),
        P(("groups", "dp")),
    )
    out_specs = P(("groups", "dp"), "tensor")

    return jax.shard_map(local, mesh=mesh, in_specs=in_specs, out_specs=out_specs, check_vma=False)
```
